32 devices in a mesh: dp: 8 (over z, x), mp: 4 (over y, core).
Axes of the slice: x: 2, y: 2, z: 4, core: 2. Of those that a mesh axis runs over, the one named last changes fastest.
Arguments:
- inputs: bfloat16 [4096, 2048], P(('dp', 'mp')), may hold values from -6 to 6
- doc_lengths: int32 [8, 8], P('dp'), may hold values from 1 to 256, 512 in all within a row
- cotangent: bfloat16 [4096, 2048], P(('dp', 'mp')), may hold values from -6 to 6
- norm_gain: float32 [2048], replicated, may hold values from 0.5 to 1.5
- query_weight: bfloat16 [2048, 2048], P(None, 'mp'), may hold values from -0.125 to 0.125
- key_weight: bfloat16 [2048, 2048], P(None, 'mp'), may hold values from -0.125 to 0.125
- value_weight: bfloat16 [2048, 2048], P(None, 'mp'), may hold values from -0.125 to 0.125
- beta_weight: bfloat16 [2048, 16], P(None, 'mp'), may hold values from -0.125 to 0.125
- gating_weight: bfloat16 [2048, 2048], P(None, 'mp'), may hold values from -0.125 to 0.125
- conv_weight: float32 [3, 4, 2048], P(None, None, 'mp'), may hold values from -3 to 3
- head_gain: float32 [128], replicated, may hold values from 0.5 to 1.5
- output_weight: bfloat16 [2048, 2048], P('mp'), may hold values from -0.1875 to 0.1875
- ffn_gain: float32 [2048], replicated, may hold values from 0.5 to 1.5
- gate_weight: bfloat16 [2048, 5632], P(None, 'mp'), may hold values from -0.125 to 0.125
- up_weight: bfloat16 [2048, 5632], P(None, 'mp'), may hold values from -0.125 to 0.125
- down_weight: bfloat16 [5632, 2048], P('mp'), may hold values from -0.109375 to 0.109375
Outputs:
- output: bfloat16 [4096, 2048], P(('dp', 'mp'))
- input_grad: float32 [4096, 2048], P(('dp', 'mp'))
- norm_gain_grad: float32 [2048], replicated
- query_grad: float32 [2048, 2048], P(None, 'mp')
- key_grad: float32 [2048, 2048], P(None, 'mp')
- value_grad: float32 [2048, 2048], P(None, 'mp')
- beta_grad: float32 [2048, 16], P(None, 'mp')
- gating_grad: float32 [2048, 2048], P(None, 'mp')
- conv_grad: float32 [3, 4, 2048], P(None, None, 'mp')
- head_gain_grad: float32 [128], replicated
- output_grad: float32 [2048, 2048], P('mp')
- ffn_gain_grad: float32 [2048], replicated
- gate_grad: float32 [2048, 5632], P(None, 'mp')
- up_grad: float32 [2048, 5632], P(None, 'mp')
- down_grad: float32 [5632, 2048], P('mp')
The draws below stay inside these ranges and needn't reach their ends.
Inputs may be any that keep to these rules, and one draw needn't show every extreme that they name: `doc_lengths`: row s lists the lengths of the documents packed in order into sequence s; each row sums to 512 and its largest entry is 256.
All inputs are finite; a program needn't handle non-finite values.
Results may differ from the reference program's by a relative error of at most 0.012.
Values may be sent and summed in bfloat16 or wider, within the bound.
A program may use at most 256 MiB of HBM per device.

```python
import math
import jax
import jax.numpy as jnp
import numpy as np
from jax import lax

D = 2048
H = 16
DK = 128
FF = 5632
CONV = 4
SPAN = 64
DOCS = 8
KD = 2048
SEQS = 1
LENGTH = 512
DOC_MOST = 256
SEQS_ALL = 8
TOKENS = 4096
N_DP = 8


def block_levels(stream_key, shape, cuts, least, top_value):
    factor_of, own = 1.0, jax.random.fold_in(stream_key, 6)
    for position, parts in cuts:
        draws = jnp.exp(jax.random.uniform(jax.random.fold_in(own, position), (parts,), jnp.float32, least / len(cuts), top_value / len(cuts)))
        factor_of = factor_of * jnp.repeat(draws, shape[position] // parts).reshape([-1 if axis == position else 1 for axis in range(len(shape))])
    return factor_of


def split_up(amount, total, bound, skew):
    weights = [(1 << 20) // math.isqrt(grade ** skew) + 1 for grade in range(2, amount + 1)]
    spare, given = total - bound - (amount - 1), [1] * (amount - 1)
    while spare > 0:
        movable = [i for i in range(amount - 1) if given[i] < bound]
        pool, left = sum([weights[i] for i in movable]), spare
        for i in movable:
            more = min(bound - given[i], max(1, left * weights[i] // pool), spare)
            given[i] = given[i] + more
            spare = spare - more
    return np.array([bound] + given)


def ragged(stream_key, count, total, limit, slope):
    if count == 2:
        one = jax.random.randint(stream_key, (), max(1, total - limit), min(limit, total - 1) + 1)
        return jnp.stack([one, total - one])
    sizes = jnp.asarray(split_up(count, total, limit, slope), jnp.int32)
    twos = (count - 1) // 2
    source_of, taker = sizes[1:1 + 2 * twos:2], sizes[2:2 + 2 * twos:2]
    slack = jnp.minimum(source_of - 1, limit - taker)
    passed = jax.random.randint(jax.random.fold_in(stream_key, 1), (twos,), 0, 1 << 20) % (slack + 1)
    sizes = sizes.at[1:1 + 2 * twos:2].set(source_of - passed).at[2:2 + 2 * twos:2].set(taker + passed)
    return sizes[jax.random.permutation(jax.random.fold_in(stream_key, 2), count)]


def gaussian(key, dims, width, limit, split=(), kind=jnp.bfloat16):
    factor_of = block_levels(key, dims, split, -0.22, 0.18) if split else 1.0
    values = jax.random.normal(key, dims, jnp.float32) * width * factor_of
    return jnp.minimum(jnp.maximum(values, -limit), limit).astype(kind)


def setup_inputs(seed: int = 0) -> dict:
    arg_keys = jax.random.split(jax.random.key(seed), 17)
    inputs = gaussian(arg_keys[0], (TOKENS, D), 1.0, 6.0, ((0, 32),))
    doc_lengths = jax.vmap(lambda own: ragged(own, DOCS, LENGTH, DOC_MOST, 2))(jax.random.split(arg_keys[1], SEQS_ALL)).reshape((SEQS_ALL, DOCS)).astype(jnp.int32)
    cotangent = gaussian(arg_keys[2], (TOKENS, D), 1.0, 6.0, ((0, 32),))
    norm_gain = jnp.clip(1.0 + 0.1 * jax.random.normal(arg_keys[3], (D,), jnp.float32), 0.5, 1.5)
    query_weight = gaussian(arg_keys[4], (D, KD), D ** -0.5, 0.125, ((1, 4),))
    key_weight = gaussian(arg_keys[5], (D, KD), D ** -0.5, 0.125, ((1, 4),))
    value_weight = gaussian(arg_keys[6], (D, KD), D ** -0.5, 0.125, ((1, 4),))
    beta_weight = gaussian(arg_keys[7], (D, H), D ** -0.5, 0.125, ((1, 4),))
    gating_weight = gaussian(arg_keys[8], (D, KD), D ** -0.5, 0.125, ((1, 4),))
    conv_weight = gaussian(arg_keys[9], (3, CONV, KD), CONV ** -0.5, 3.0, ((2, 4),), jnp.float32)
    head_gain = jnp.clip(1.0 + 0.1 * jax.random.normal(arg_keys[10], (DK,), jnp.float32), 0.5, 1.5)
    output_weight = gaussian(arg_keys[11], (KD, D), (KD // 2) ** -0.5, 0.1875, ((0, 4),))
    ffn_gain = jnp.clip(1.0 + 0.1 * jax.random.normal(arg_keys[12], (D,), jnp.float32), 0.5, 1.5)
    gate_weight = gaussian(arg_keys[13], (D, FF), D ** -0.5, 0.125, ((1, 4),))
    up_weight = gaussian(arg_keys[14], (D, FF), D ** -0.5, 0.125, ((1, 4),))
    down_weight = gaussian(arg_keys[15], (FF, D), (FF // 2) ** -0.5, 0.109375, ((0, 4),))
    return dict(inputs=inputs, doc_lengths=doc_lengths, cotangent=cotangent, norm_gain=norm_gain, query_weight=query_weight, key_weight=key_weight, value_weight=value_weight, beta_weight=beta_weight, gating_weight=gating_weight, conv_weight=conv_weight, head_gain=head_gain, output_weight=output_weight, ffn_gain=ffn_gain, gate_weight=gate_weight, up_weight=up_weight, down_weight=down_weight)


EPS_NORM = 1e-06
EPS_UNIT = 1e-06
EPS_HEAD = 0.05
PRECISE = lax.Precision.HIGHEST

@jax.custom_vjp
def low(v):
    return lax.optimization_barrier(v.astype(jnp.bfloat16)).astype(jnp.float32)

@jax.custom_vjp
def low_back(v):
    return v

def low_keep(v):
    return (low(v), None)

def low_pass(kept, grad):
    return (grad,)

def back_keep(v):
    return (v, None)

def back_low(kept, grad):
    return (low(grad),)
low.defvjp(low_keep, low_pass)
low_back.defvjp(back_keep, back_low)

def sigmoid_linear(values):
    return values * jax.nn.sigmoid(values)

def scaled_norm(values, gains, epsilon):
    return values * lax.rsqrt(lax.optimization_barrier(jnp.mean(values * values, axis=-1, keepdims=True)) + epsilon) * gains

def exact_dot(left, right):
    return jnp.dot(left, right, precision=PRECISE)

def doc_index(lengths, length):
    starts = (jnp.cumsum(lengths, axis=1) - lengths).astype(jnp.int32)
    places = jnp.arange(length, dtype=jnp.int32)
    within = lax.optimization_barrier(jnp.sum((starts[:, :, None] <= places[None, None, :]).astype(jnp.int32), axis=1)).astype(jnp.int32) - 1
    offsets = jnp.arange(lengths.shape[0], dtype=jnp.int32)[:, None] * lengths.shape[1]
    return (within + offsets).astype(jnp.int32).reshape(-1)

def make_masks(doc_ids, ftype):
    masks = []
    for lag_step in range(CONV):
        before = jnp.concatenate([jnp.full((lag_step,), -1, jnp.int32), doc_ids[:doc_ids.shape[0] - lag_step]])
        masks.append((doc_ids == before).astype(ftype)[:, None])
    return masks

def lagged(values, lag_step):
    if lag_step == 0:
        return values
    padding = jnp.zeros((lag_step,) + values.shape[1:], values.dtype)
    return jnp.concatenate([padding, values[:values.shape[0] - lag_step]], axis=0)

def conv_apply(values, conv_taps, masks):
    summed = conv_taps[0] * values * masks[0]
    for lag_step in range(1, CONV):
        summed = summed + conv_taps[lag_step] * lagged(values, lag_step) * masks[lag_step]
    return summed

def unit_rows(values):
    return values * lax.rsqrt(lax.optimization_barrier(jnp.sum(values * values, axis=-1, keepdims=True)) + EPS_UNIT)

def delta_rule(query_all, key_all, value_all, rates, doc_ids):
    total_rows = doc_ids.shape[0]
    count = total_rows // SPAN

    def blocked(values):
        return jnp.transpose(values.reshape(count, SPAN, H, DK), (0, 2, 1, 3))
    rate_blocks = jnp.transpose(rates.reshape(count, SPAN, H), (0, 2, 1))
    prior = jnp.concatenate([jnp.full((1,), -1, jnp.int32), doc_ids[:-1]]).reshape(count, SPAN)[:, 0]

    def block_step(carry_state, block):
        query_rows, key_rows, value_rows, rate_rows, block_ids, before = block
        ftype = key_rows.dtype
        row_ids = lax.broadcasted_iota(jnp.int32, (SPAN, SPAN), 0)
        col_ids = lax.broadcasted_iota(jnp.int32, (SPAN, SPAN), 1)
        sameness = block_ids[:, None] == block_ids[None, :]
        strict = (sameness & (row_ids > col_ids)).astype(ftype)
        inclusive = (sameness & (row_ids >= col_ids)).astype(ftype)
        opening = (block_ids == before).astype(ftype)[None, :, None]
        closing = (block_ids == block_ids[SPAN - 1]).astype(ftype)[None, :, None]
        carried = (block_ids[SPAN - 1] == before).astype(ftype)
        gram_mat = jnp.einsum('hik,hjk->hij', key_rows, key_rows, precision=PRECISE)
        lower_mat = jnp.eye(SPAN, dtype=ftype) + rate_rows[:, :, None] * gram_mat * strict
        stacked = jnp.concatenate([key_rows, value_rows], axis=-1)
        solved = jax.scipy.linalg.solve_triangular(lower_mat, rate_rows[:, :, None] * stacked, lower=True, unit_diagonal=True)
        new_value = solved[..., DK:] - opening * jnp.einsum('hck,hvk->hcv', solved[..., :DK], carry_state, precision=PRECISE)
        probes = jnp.einsum('hik,hjk->hij', query_rows, key_rows, precision=PRECISE) * inclusive
        outputs = opening * jnp.einsum('hck,hvk->hcv', query_rows, carry_state, precision=PRECISE) + jnp.einsum('hij,hjv->hiv', probes, new_value, precision=PRECISE)
        updated = carried * carry_state + jnp.einsum('hcv,hck->hvk', closing * new_value, key_rows, precision=PRECISE)
        return (updated, outputs)
    start_state = jnp.zeros((H, DK, DK), query_all.dtype)
    final_state, outputs = lax.scan(jax.checkpoint(block_step), start_state, (blocked(query_all), blocked(key_all), blocked(value_all), rate_blocks, doc_ids.reshape(count, SPAN), prior))
    return jnp.transpose(outputs, (0, 2, 1, 3)).reshape(total_rows, H, DK)

def layer_forward(params, inputs_f, doc_ids, masks):
    norm_gain, query_weight, key_weight, value_weight, beta_weight, gating_weight, conv_weight, head_gain, output_weight, ffn_gain, gate_weight, up_weight, down_weight = params
    total_rows = inputs_f.shape[0]
    normed = low(scaled_norm(inputs_f, norm_gain, EPS_NORM))
    query_proj = low_back(exact_dot(normed, query_weight))
    key_proj = low_back(exact_dot(normed, key_weight))
    value_proj = low_back(exact_dot(normed, value_weight))
    beta_logit = low_back(exact_dot(normed, beta_weight))
    gate_proj = low_back(exact_dot(normed, gating_weight))
    query_act = sigmoid_linear(conv_apply(query_proj, conv_weight[0], masks)).reshape(total_rows, H, DK)
    key_act = sigmoid_linear(conv_apply(key_proj, conv_weight[1], masks)).reshape(total_rows, H, DK)
    value_act = sigmoid_linear(conv_apply(value_proj, conv_weight[2], masks)).reshape(total_rows, H, DK)
    query_low = low(unit_rows(query_act))
    key_low = low(unit_rows(key_act))
    value_low = low(value_act)
    betas = jax.nn.sigmoid(beta_logit)
    mixed = delta_rule(query_low, key_low, value_low, betas, doc_ids)
    gate_act = sigmoid_linear(gate_proj).reshape(total_rows, H, DK)
    mixer_in = low((scaled_norm(mixed, head_gain, EPS_HEAD) * gate_act).reshape(total_rows, H * DK))
    attended = low_back(exact_dot(mixer_in, output_weight))
    middle = inputs_f + attended
    ffn_in = low(scaled_norm(middle, ffn_gain, EPS_NORM))
    gate_pre = low_back(exact_dot(ffn_in, gate_weight))
    up_pre = low_back(exact_dot(ffn_in, up_weight))
    hidden = low(sigmoid_linear(gate_pre) * up_pre)
    return middle + exact_dot(hidden, down_weight)

def reference(inputs, doc_lengths, cotangent, norm_gain, query_weight, key_weight, value_weight, beta_weight, gating_weight, conv_weight, head_gain, output_weight, ffn_gain, gate_weight, up_weight, down_weight):
    params = tuple((weight.astype(jnp.float32) for weight in (norm_gain, query_weight, key_weight, value_weight, beta_weight, gating_weight, conv_weight, head_gain, output_weight, ffn_gain, gate_weight, up_weight, down_weight)))
    group_rows = TOKENS // N_DP
    in_groups = inputs.astype(jnp.float32).reshape(N_DP, group_rows, D)
    cot_groups = cotangent.astype(jnp.float32).reshape(N_DP, group_rows, D)
    len_groups = doc_lengths.reshape(N_DP, SEQS, DOCS)

    def per_group(totals, item):
        group_in, group_cot, group_len = item
        doc_ids = doc_index(group_len, LENGTH)
        masks = make_masks(doc_ids, group_in.dtype)
        result, pullback = jax.vjp(lambda weights, values: layer_forward(weights, values, doc_ids, masks), params, group_in)
        d_params, d_inputs = pullback(group_cot)
        totals = jax.tree.map(lambda left, right: left + right, totals, d_params)
        return (totals, (result.astype(jnp.bfloat16), d_inputs))
    zero_sums = jax.tree.map(jnp.zeros_like, params)
    totals, (outputs, d_inputs) = lax.scan(per_group, zero_sums, (in_groups, cot_groups, len_groups))
    return (outputs.reshape(TOKENS, D), d_inputs.reshape(TOKENS, D), totals[0], totals[1], totals[2], totals[3], totals[4], totals[5], totals[6], totals[7], totals[8], totals[9], totals[10], totals[11], totals[12])
```

```python
import functools

import jax
import jax.numpy as jnp
from jax import lax
from jax.experimental import pallas as pl
from jax.experimental.pallas import tpu as pltpu
from jax.sharding import PartitionSpec as P

DK = 128
CONV = 4
SPAN = 128
PAD = 8


EPS_NORM = 1e-06
EPS_UNIT = 1e-06
EPS_HEAD = 0.05
LOW = jnp.bfloat16
FULL = jnp.float32


def sigmoid(values):
    return 1.0 / (1.0 + jnp.exp(-values))


def parts_of(values):
    high = values.astype(LOW)
    return (high, (values - high.astype(FULL)).astype(LOW))


def product(left, right, left_dim=1, right_dim=0):
    dims = (((left_dim,), (right_dim,)), ((), ()))
    right_free = 1 - right_dim
    width = right[0].shape[right_free]
    if len(left) == 2:
        left_all = jnp.concatenate(left, axis=left_dim)
        first = jnp.concatenate([right[0], right[0]], axis=right_dim)
    else:
        left_all, first = left[0], right[0]
    if len(right) == 1:
        return lax.dot_general(left_all, first, dims, preferred_element_type=FULL)
    second = right[1]
    if len(left) == 2:
        second = jnp.concatenate([second, jnp.zeros_like(second)], axis=right_dim)
    both = lax.dot_general(
        left_all,
        jnp.concatenate([first, second], axis=right_free),
        dims,
        preferred_element_type=FULL,
    )
    return both[:, :width] + both[:, width:]


def lag_rows(stacked, lag_step):
    if lag_step == 0:
        return stacked[PAD:]
    return pltpu.roll(stacked, lag_step, axis=0)[PAD:]


def lead_rows(stacked, lag_step):
    rows = stacked.shape[0]
    if lag_step == 0:
        return stacked[: rows - PAD]
    return pltpu.roll(stacked, rows - lag_step, axis=0)[: rows - PAD]


def with_earlier(ref, start, columns):
    before = pl.multiple_of(jnp.maximum(start - PAD, 0), PAD)
    return jnp.concatenate(
        [ref[pl.ds(before, PAD), columns], ref[pl.ds(start, SPAN), columns]], axis=0
    )


def block_masks(meta_ref, ids_ref, start, index):
    ids_col = meta_ref[pl.ds(start, SPAN), 0:1]
    ids_row = ids_ref[pl.ds(index, 1), :]
    row_ids = lax.broadcasted_iota(jnp.int32, (SPAN, SPAN), 0)
    col_ids = lax.broadcasted_iota(jnp.int32, (SPAN, SPAN), 1)
    same = ids_col == ids_row
    strict = jnp.where(same & (row_ids > col_ids), 1.0, 0.0)
    inclusive = jnp.where(same & (row_ids >= col_ids), 1.0, 0.0)
    return strict, inclusive, row_ids, col_ids


def spread(meta_ref, start, column, rows=SPAN):
    return jnp.broadcast_to(meta_ref[pl.ds(start, rows), column : column + 1], (rows, DK))


def inverse_lower(lower, row_ids, col_ids):
    size = lower.shape[0]
    step = 1
    result = jnp.where(row_ids == col_ids, 1.0, 0.0)
    while step < size:
        pair = (row_ids // (2 * step) == col_ids // (2 * step)) & (
            row_ids // step != col_ids // step
        )
        link = jnp.where(pair, lower, 0.0)
        if step == 1:
            result = result - link
        else:
            result_parts = parts_of(result)
            inner = product(parts_of(link), result_parts)
            result = result - product(result_parts, parts_of(inner))
        step = 2 * step
    return result


def mixer_forward(
    head_count,
    query_ref,
    key_ref,
    value_ref,
    gate_ref,
    logit_ref,
    taps_ref,
    gain_ref,
    meta_ref,
    ids_ref,
    mixer_ref,
    conv_ref,
    solve_ref,
    w_ref,
    u_ref,
    new_ref,
    mixed_ref,
    states_ref,
    state,
):
    state[...] = jnp.zeros_like(state)
    gain = gain_ref[...]

    def step(index, carry):
        start = pl.multiple_of(index * SPAN, SPAN)
        rows = pl.ds(start, SPAN)
        strict, inclusive, row_ids, col_ids = block_masks(meta_ref, ids_ref, start, index)
        tap_masks = [None] + [spread(meta_ref, start, lag_step) for lag_step in range(1, CONV)]
        opening = spread(meta_ref, start, 4)
        closing = spread(meta_ref, start, 5)
        carried = spread(meta_ref, start, 6)
        betas = sigmoid(logit_ref[rows, :])
        for head in range(head_count):
            columns = slice(head * DK, (head + 1) * DK)
            acts = []
            for which, ref in enumerate((query_ref, key_ref, value_ref)):
                stacked = with_earlier(ref, start, columns)
                tap = 4 * which
                total = taps_ref[tap : tap + 1, columns] * lag_rows(stacked, 0)
                for lag_step in range(1, CONV):
                    total = total + (
                        taps_ref[tap + lag_step : tap + lag_step + 1, columns]
                        * lag_rows(stacked, lag_step)
                        * tap_masks[lag_step]
                    )
                conv_ref[which, rows, columns] = total
                acts.append(total * sigmoid(total))
            unit = [
                act * lax.rsqrt(jnp.sum(act * act, axis=-1, keepdims=True) + EPS_UNIT)
                for act in acts[:2]
            ]
            queries, keys, values = unit[0].astype(LOW), unit[1].astype(LOW), acts[2].astype(LOW)
            beta = jnp.broadcast_to(betas[:, head : head + 1], (SPAN, DK))
            gram = product((keys,), (keys,), 1, 1)
            solve = inverse_lower(beta * gram * strict, row_ids, col_ids)
            solve_ref[head, rows, :] = solve
            solve_parts = parts_of(solve)
            w_rows = product(solve_parts, parts_of(beta * keys.astype(FULL)))
            u_rows = product(solve_parts, parts_of(beta * values.astype(FULL)))
            w_ref[rows, columns] = w_rows
            u_ref[rows, columns] = u_rows
            probes = product((queries,), (keys,), 1, 1) * inclusive
            before = state[head]
            states_ref[head, rows, :] = before
            before_parts = parts_of(before)
            new_value = u_rows - opening * product(parts_of(w_rows), before_parts)
            new_ref[rows, columns] = new_value
            mixed = opening * product((queries,), before_parts) + product(
                parts_of(probes), parts_of(new_value)
            )
            mixed_ref[rows, columns] = mixed
            state[head] = carried * before + product(
                (keys,), parts_of(closing * new_value), 0, 0
            )
            scale = lax.rsqrt(jnp.mean(mixed * mixed, axis=-1, keepdims=True) + EPS_HEAD)
            gates = gate_ref[rows, columns]
            mixer_ref[rows, columns] = (mixed * scale * gain * (gates * sigmoid(gates))).astype(LOW)
        return carry

    lax.fori_loop(0, query_ref.shape[0] // SPAN, step, 0)


def mixer_backward(
    head_count,
    d_mixer_ref,
    query_ref,
    key_ref,
    value_ref,
    gate_ref,
    logit_ref,
    taps_ref,
    gain_ref,
    meta_ref,
    ids_ref,
    conv_ref,
    solve_ref,
    w_ref,
    u_ref,
    new_ref,
    mixed_ref,
    states_ref,
    d_query_ref,
    d_key_ref,
    d_value_ref,
    d_gate_ref,
    d_logit_ref,
    d_taps_ref,
    d_gain_ref,
    d_state,
    later,
):
    d_state[...] = jnp.zeros_like(d_state)
    later[...] = jnp.zeros_like(later)
    d_taps_ref[...] = jnp.zeros_like(d_taps_ref)
    d_gain_ref[...] = jnp.zeros_like(d_gain_ref)
    gain = gain_ref[...]
    total_rows = query_ref.shape[0]
    count = total_rows // SPAN

    def step(back, carry):
        index = count - 1 - back
        start = pl.multiple_of(index * SPAN, SPAN)
        rows = pl.ds(start, SPAN)
        strict, inclusive, row_ids, col_ids = block_masks(meta_ref, ids_ref, start, index)
        after = pl.multiple_of(jnp.minimum(start + SPAN, total_rows - PAD), PAD)
        tap_masks = [None] + [
            jnp.concatenate(
                [
                    spread(meta_ref, start, lag_step),
                    spread(meta_ref, after, lag_step, PAD),
                ],
                axis=0,
            )
            for lag_step in range(1, CONV)
        ]
        opening = spread(meta_ref, start, 4)
        closing = spread(meta_ref, start, 5)
        carried = spread(meta_ref, start, 6)
        betas = sigmoid(logit_ref[rows, :])
        lanes = lax.broadcasted_iota(jnp.int32, (SPAN, DK), 1)
        d_logits = jnp.zeros((SPAN, DK), FULL)
        d_gain = jnp.zeros((1, DK), FULL)
        for head in range(head_count):
            columns = slice(head * DK, (head + 1) * DK)
            d_mixer = d_mixer_ref[rows, columns]
            gates = gate_ref[rows, columns]
            logistic = sigmoid(gates)
            mixed = mixed_ref[rows, columns]
            scale = lax.rsqrt(jnp.mean(mixed * mixed, axis=-1, keepdims=True) + EPS_HEAD)
            unit_mixed = mixed * scale
            d_gate_ref[rows, columns] = (
                d_mixer * (unit_mixed * gain) * (logistic * (1.0 + gates * (1.0 - logistic)))
            ).astype(LOW)
            d_normed = d_mixer * (gates * logistic)
            d_gain = d_gain + jnp.sum(d_normed * unit_mixed, axis=0, keepdims=True)
            weighted = d_normed * gain
            inner = jnp.mean(weighted * mixed, axis=-1, keepdims=True)
            d_out = scale * weighted - mixed * (scale * scale * scale) * inner
            convs = [conv_ref[which, rows, columns] for which in range(3)]
            logistics = [sigmoid(conv) for conv in convs]
            acts = [conv * logistic for conv, logistic in zip(convs, logistics)]
            scales = [
                lax.rsqrt(jnp.sum(act * act, axis=-1, keepdims=True) + EPS_UNIT)
                for act in acts[:2]
            ]
            queries = (acts[0] * scales[0]).astype(LOW)
            keys = (acts[1] * scales[1]).astype(LOW)
            values = acts[2].astype(LOW)
            beta = jnp.broadcast_to(betas[:, head : head + 1], (SPAN, DK))
            gram = product((keys,), (keys,), 1, 1)
            probes = product((queries,), (keys,), 1, 1) * inclusive
            solve_parts = parts_of(solve_ref[head, rows, :])
            w_parts = parts_of(w_ref[rows, columns])
            u_parts = parts_of(u_ref[rows, columns])
            new_value = new_ref[rows, columns]
            new_parts = parts_of(new_value)
            before_parts = parts_of(states_ref[head, rows, :])
            d_after = d_state[head]
            d_after_parts = parts_of(d_after)
            d_out_parts = parts_of(d_out)
            d_new = product(parts_of(probes), d_out_parts, 0, 0) + closing * product(
                (keys,), d_after_parts
            )
            opened_out = opening * d_out
            opened_new = opening * d_new
            d_state[head] = (
                carried * d_after
                + product((queries,), parts_of(opened_out), 0, 0)
                - product(w_parts, parts_of(opened_new), 0, 0)
            )
            d_probe = product(d_out_parts, new_parts, 1, 1) * inclusive
            d_probe_parts = parts_of(d_probe)
            d_query = product(d_probe_parts, (keys,)) + product(
                parts_of(opened_out), before_parts, 1, 1
            )
            d_key = product(d_probe_parts, (queries,), 0, 0) + closing * product(
                new_parts, d_after_parts, 1, 1
            )
            d_w = -product(parts_of(opened_new), before_parts, 1, 1)
            right_w = product(solve_parts, parts_of(d_w), 0, 0)
            right_u = product(solve_parts, parts_of(d_new), 0, 0)
            d_lower = (
                -(
                    product(parts_of(right_w), w_parts, 1, 1)
                    + product(parts_of(right_u), u_parts, 1, 1)
                )
                * strict
            )
            d_beta = jnp.sum(
                right_w * keys.astype(FULL) + right_u * values.astype(FULL) + d_lower * gram,
                axis=-1,
                keepdims=True,
            )
            beta_col = betas[:, head : head + 1]
            d_logits = d_logits + jnp.where(
                lanes == head, d_beta * beta_col * (1.0 - beta_col), 0.0
            )
            d_gram_parts = parts_of(beta * d_lower)
            d_key = (
                d_key
                + beta * right_w
                + product(d_gram_parts, (keys,))
                + product(d_gram_parts, (keys,), 0, 0)
            )
            d_value = beta * right_u
            d_acts = [
                scales[which] * grads
                - acts[which]
                * (scales[which] * scales[which] * scales[which])
                * jnp.sum(grads * acts[which], axis=-1, keepdims=True)
                for which, grads in enumerate((d_query, d_key))
            ] + [d_value]
            for which, (ref, out_ref) in enumerate(
                ((query_ref, d_query_ref), (key_ref, d_key_ref), (value_ref, d_value_ref))
            ):
                logistic = logistics[which]
                d_conv = d_acts[which] * (logistic * (1.0 + convs[which] * (1.0 - logistic)))
                tap = 4 * which
                following = jnp.concatenate([d_conv, later[which, :, columns]], axis=0)
                earlier = with_earlier(ref, start, columns)
                later[which, :, columns] = d_conv[:PAD]
                total = taps_ref[tap : tap + 1, columns] * d_conv
                d_taps = [jnp.sum(d_conv * lag_rows(earlier, 0), axis=0, keepdims=True)]
                for lag_step in range(1, CONV):
                    masked = following * tap_masks[lag_step]
                    total = total + taps_ref[
                        tap + lag_step : tap + lag_step + 1, columns
                    ] * lead_rows(masked, lag_step)
                    d_taps.append(
                        jnp.sum(
                            masked[:SPAN] * lag_rows(earlier, lag_step), axis=0, keepdims=True
                        )
                    )
                out_ref[rows, columns] = total.astype(LOW)
                for lag_step in range(CONV):
                    place = slice(tap + lag_step, tap + lag_step + 1)
                    d_taps_ref[place, columns] = d_taps_ref[place, columns] + d_taps[lag_step]
        d_logit_ref[rows, :] = d_logits.astype(LOW)
        d_gain_ref[...] = d_gain_ref[...] + d_gain
        return carry

    lax.fori_loop(0, count, step, 0)


def whole_blocks(count):
    return [pl.BlockSpec(memory_space=pltpu.VMEM)] * count


def run_mixer_forward(projections, logits, taps, gain, meta, ids):
    rows, width = projections[0].shape
    head_count = width // DK
    tall = jax.ShapeDtypeStruct((rows, width), FULL)
    square = jax.ShapeDtypeStruct((head_count, rows, DK), FULL)
    return pl.pallas_call(
        functools.partial(mixer_forward, head_count),
        out_shape=(
            jax.ShapeDtypeStruct((rows, width), LOW),
            jax.ShapeDtypeStruct((3, rows, width), FULL),
            square,
            tall,
            tall,
            tall,
            tall,
            square,
        ),
        in_specs=whole_blocks(9),
        out_specs=tuple(whole_blocks(8)),
        scratch_shapes=[pltpu.VMEM((head_count, DK, DK), FULL)],
        compiler_params=pltpu.CompilerParams(vmem_limit_bytes=56 * 1024 * 1024),
        name="mixer_forward",
    )(*projections, logits, taps, gain, meta, ids)


def run_mixer_backward(d_mixer, projections, logits, taps, gain, meta, ids, kept):
    rows, width = projections[0].shape
    head_count = width // DK
    low = jax.ShapeDtypeStruct((rows, width), LOW)
    return pl.pallas_call(
        functools.partial(mixer_backward, head_count),
        out_shape=(
            low,
            low,
            low,
            low,
            jax.ShapeDtypeStruct((rows, DK), LOW),
            jax.ShapeDtypeStruct(taps.shape, FULL),
            jax.ShapeDtypeStruct((1, DK), FULL),
        ),
        in_specs=whole_blocks(17),
        out_specs=tuple(whole_blocks(7)),
        scratch_shapes=[
            pltpu.VMEM((head_count, DK, DK), FULL),
            pltpu.VMEM((3, PAD, width), FULL),
        ],
        compiler_params=pltpu.CompilerParams(vmem_limit_bytes=56 * 1024 * 1024),
        name="mixer_backward",
    )(d_mixer, *projections, logits, taps, gain, meta, ids, *kept)


def document_tables(doc_ids):
    rows = doc_ids.shape[0]
    columns = [doc_ids.astype(FULL)]
    for lag_step in range(1, CONV):
        before = jnp.concatenate(
            [jnp.full((lag_step,), -1, jnp.int32), doc_ids[: rows - lag_step]]
        )
        columns.append((doc_ids == before).astype(FULL))
    blocks = doc_ids.reshape(rows // SPAN, SPAN)
    prior = jnp.concatenate([jnp.full((1,), -1, jnp.int32), blocks[:-1, SPAN - 1]])[:, None]
    last = blocks[:, SPAN - 1 :]
    columns.append((blocks == prior).astype(FULL).reshape(-1))
    columns.append((blocks == last).astype(FULL).reshape(-1))
    columns.append(jnp.broadcast_to(last == prior, blocks.shape).astype(FULL).reshape(-1))
    columns.append(jnp.zeros((rows,), FULL))
    return jnp.stack(columns, axis=1), blocks.astype(FULL)


def by_pairs(values, bit):
    count = lax.axis_size("mp")
    return lax.ppermute(values, "mp", [(here, here ^ bit) for here in range(count)])


def gather_rows(values):
    if lax.axis_size("mp") != 4:
        return lax.all_gather(values, "mp", axis=0, tiled=True)
    here = lax.axis_index("mp")
    other_core = by_pairs(values, 1)
    other_chip = by_pairs(values, 2)
    far = by_pairs(other_chip, 1)
    odd_core, odd_chip = here % 2 == 1, here // 2 == 1
    near_pair = jnp.where(
        odd_core,
        jnp.concatenate([other_core, values]),
        jnp.concatenate([values, other_core]),
    )
    far_pair = jnp.where(
        odd_core, jnp.concatenate([far, other_chip]), jnp.concatenate([other_chip, far])
    )
    return jnp.where(
        odd_chip, jnp.concatenate([far_pair, near_pair]), jnp.concatenate([near_pair, far_pair])
    )


def scatter_sum(values):
    if lax.axis_size("mp") != 4:
        return lax.psum_scatter(values, "mp", scatter_dimension=0, tiled=True)
    here = lax.axis_index("mp")
    core, chip = here % 2, here // 2
    quarters = values.reshape(2, 2, values.shape[0] // 4, values.shape[1])
    sent = lax.dynamic_index_in_dim(quarters, 1 - core, 1, keepdims=False).astype(LOW)
    kept = lax.dynamic_index_in_dim(quarters, core, 1, keepdims=False)
    halves = kept + by_pairs(sent, 1).astype(FULL)
    sent = lax.dynamic_index_in_dim(halves, 1 - chip, 0, keepdims=False).astype(LOW)
    kept = lax.dynamic_index_in_dim(halves, chip, 0, keepdims=False)
    return kept + by_pairs(sent, 2).astype(FULL)


def inverse_root(values, epsilon):
    return lax.rsqrt(jnp.mean(values * values, axis=-1, keepdims=True) + epsilon)


def norm_back(values, scales, gains, grads):
    weighted = grads * gains
    inner_sum = jnp.mean(weighted * values, axis=-1, keepdims=True)
    return scales * weighted - values * (scales * scales * scales) * inner_sum


def sigmoid_linear(values):
    return values * sigmoid(values)


def sigmoid_slope(values):
    logistic = sigmoid(values)
    return logistic * (1.0 + values * (1.0 - logistic))


def doc_index(lengths, length):
    starts = jnp.cumsum(lengths, axis=1) - lengths
    places = jnp.arange(length, dtype=jnp.int32)
    within = jnp.sum((starts[:, :, None] <= places[None, None, :]).astype(jnp.int32), axis=1) - 1
    offsets = jnp.arange(lengths.shape[0], dtype=jnp.int32)[:, None] * lengths.shape[1]
    return (within + offsets).reshape(-1)


def dot_full(equation, left, right):
    return jnp.einsum(equation, left, right, preferred_element_type=FULL)


def on_device(
    inputs,
    doc_lengths,
    cotangent,
    norm_gain,
    query_weight,
    key_weight,
    value_weight,
    beta_weight,
    gating_weight,
    conv_weight,
    head_gain,
    output_weight,
    ffn_gain,
    gate_weight,
    up_weight,
    down_weight,
):
    local_rows = inputs.shape[0]
    group_rows = local_rows * lax.axis_size("mp")
    width = query_weight.shape[1]
    head_count = width // DK
    meta, ids = document_tables(doc_index(doc_lengths, group_rows // doc_lengths.shape[0]))
    taps = conv_weight.reshape(3 * CONV, width)
    gain_row = head_gain[None, :]

    residual_in = inputs.astype(FULL)
    scale_one = inverse_root(residual_in, EPS_NORM)
    normed = gather_rows((residual_in * scale_one * norm_gain).astype(LOW))
    grad_rows = gather_rows(cotangent)
    weights = (query_weight, key_weight, value_weight, gating_weight)
    projections = tuple(dot_full("td,df->tf", normed, weight) for weight in weights)
    logits = dot_full("td,df->tf", normed, beta_weight)
    mixer_low, *kept = run_mixer_forward(projections, logits, taps, gain_row, meta, ids)
    attended = scatter_sum(dot_full("tf,fd->td", mixer_low, output_weight))
    residual_mid = residual_in + attended
    scale_two = inverse_root(residual_mid, EPS_NORM)
    ffn_input = gather_rows((residual_mid * scale_two * ffn_gain).astype(LOW))

    gate_pre = dot_full("td,df->tf", ffn_input, gate_weight)
    up_pre = dot_full("td,df->tf", ffn_input, up_weight)
    d_hidden = dot_full("td,fd->tf", grad_rows, down_weight)
    gate_swish = sigmoid_linear(gate_pre)
    hidden_low = (gate_swish * up_pre).astype(LOW)
    d_gate_low = (d_hidden * up_pre * sigmoid_slope(gate_pre)).astype(LOW)
    d_up_low = (d_hidden * gate_swish).astype(LOW)
    d_ffn_norm = scatter_sum(
        dot_full("tf,df->td", d_gate_low, gate_weight) + dot_full("tf,df->td", d_up_low, up_weight)
    )
    ffn_out = scatter_sum(dot_full("tf,fd->td", hidden_low, down_weight))
    output = (residual_mid + ffn_out).astype(LOW)
    d_down = dot_full("tf,td->fd", hidden_low, grad_rows)
    d_gate_w = dot_full("td,tf->df", ffn_input, d_gate_low)
    d_up_w = dot_full("td,tf->df", ffn_input, d_up_low)

    d_mid = cotangent.astype(FULL) + norm_back(residual_mid, scale_two, ffn_gain, d_ffn_norm)
    ffn_gain_part = jnp.sum(d_ffn_norm * residual_mid * scale_two, axis=0)
    mid_rows = gather_rows(d_mid.astype(LOW))
    d_output_w = dot_full("tf,td->fd", mixer_low, mid_rows)
    d_mixer = dot_full("td,fd->tf", mid_rows, output_weight)
    *low_grads, d_logits, d_taps, head_gain_part = run_mixer_backward(
        d_mixer, projections, logits, taps, gain_row, meta, ids, kept
    )
    d_logits = d_logits[:, :head_count]
    summed = dot_full("tf,df->td", d_logits, beta_weight)
    for grads, weight in zip(low_grads, weights):
        summed = summed + dot_full("tf,df->td", grads, weight)
    d_normed = scatter_sum(summed)
    input_grad = d_mid + norm_back(residual_in, scale_one, norm_gain, d_normed)
    norm_gain_part = jnp.sum(d_normed * residual_in * scale_one, axis=0)
    proj_grads = [dot_full("td,tf->df", normed, grads).astype(LOW) for grads in low_grads]
    d_beta_w = dot_full("td,tf->df", normed, d_logits)

    gains = jnp.concatenate([norm_gain_part, ffn_gain_part, head_gain_part[0]])
    gains = lax.psum(gains, "mp")
    small = jnp.concatenate([d_beta_w.reshape(-1), d_taps.reshape(-1), gains])
    size = small.shape[0]
    padded = -(-size // (16 * 512)) * 16 * 512
    small = jnp.pad(small, (0, padded - size)).reshape(-1, 512).astype(LOW)
    wide = [grads.astype(LOW) for grads in (d_gate_w, d_up_w, d_down)]
    narrow = proj_grads + [d_output_w.astype(LOW), small]
    d_gate_w, d_up_w, d_down, *proj_grads, d_output_w, small = [
        grads.astype(FULL) for grads in lax.psum(tuple(wide + narrow), "dp")
    ]
    small = small.reshape(-1)
    beta_size, taps_size = d_beta_w.size, taps.size
    d_beta_w = small[:beta_size].reshape(d_beta_w.shape)
    d_conv = small[beta_size : beta_size + taps_size].reshape(conv_weight.shape)
    gains = small[beta_size + taps_size : size]
    features = inputs.shape[1]
    return (
        output,
        input_grad,
        gains[:features],
        proj_grads[0],
        proj_grads[1],
        proj_grads[2],
        d_beta_w,
        proj_grads[3],
        d_conv,
        gains[2 * features :],
        d_output_w,
        gains[features : 2 * features],
        d_gate_w,
        d_up_w,
        d_down,
    )


def solution(mesh):
    rows, columns = P(("dp", "mp"), None), P(None, "mp")
    return jax.shard_map(
        on_device,
        mesh=mesh,
        in_specs=(
            rows,
            P("dp", None),
            rows,
            P(),
            columns,
            columns,
            columns,
            columns,
            columns,
            P(None, None, "mp"),
            P(),
            P("mp", None),
            P(),
            columns,
            columns,
            P("mp", None),
        ),
        out_specs=(
            rows,
            rows,
            P(),
            columns,
            columns,
            columns,
            columns,
            columns,
            P(None, None, "mp"),
            P(),
            P("mp", None),
            P(),
            columns,
            columns,
            P("mp", None),
        ),
        check_vma=False,
    )
```

```python
import functools

import jax
import jax.numpy as jnp
from jax import lax
from jax.experimental import pallas as pl
from jax.experimental.pallas import tpu as pltpu
from jax.sharding import PartitionSpec as P

DK = 128
CONV = 4
SPAN = 128
PAD = 8
ROWS_MOST = 8192


EPS_NORM = 1e-06
EPS_UNIT = 1e-06
EPS_HEAD = 0.05
LOW = jnp.bfloat16
FULL = jnp.float32


def sigmoid(values):
    return 1.0 / (1.0 + jnp.exp(-values))


def parts_of(values):
    high = values.astype(LOW)
    return (high, (values - high.astype(FULL)).astype(LOW))


def product(left, right, left_dim=1, right_dim=0):
    dims = (((left_dim,), (right_dim,)), ((), ()))
    right_free = 1 - right_dim
    width = right[0].shape[right_free]
    if len(left) == 2:
        left_all = jnp.concatenate(left, axis=left_dim)
        first = jnp.concatenate([right[0], right[0]], axis=right_dim)
    else:
        left_all, first = left[0], right[0]
    if len(right) == 1:
        return lax.dot_general(left_all, first, dims, preferred_element_type=FULL)
    second = right[1]
    if len(left) == 2:
        second = jnp.concatenate([second, jnp.zeros_like(second)], axis=right_dim)
    both = lax.dot_general(
        left_all,
        jnp.concatenate([first, second], axis=right_free),
        dims,
        preferred_element_type=FULL,
    )
    return both[:, :width] + both[:, width:]


def lag_rows(stacked, lag_step):
    if lag_step == 0:
        return stacked[PAD:]
    return pltpu.roll(stacked, lag_step, axis=0)[PAD:]


def lead_rows(stacked, lag_step):
    rows = stacked.shape[0]
    if lag_step == 0:
        return stacked[: rows - PAD]
    return pltpu.roll(stacked, rows - lag_step, axis=0)[: rows - PAD]


def with_earlier(ref, start, columns):
    before = pl.multiple_of(jnp.maximum(start - PAD, 0), PAD)
    return jnp.concatenate(
        [ref[pl.ds(before, PAD), columns], ref[pl.ds(start, SPAN), columns]], axis=0
    )


def block_masks(meta_ref, ids_ref, start, index):
    ids_col = meta_ref[pl.ds(start, SPAN), 0:1]
    ids_row = ids_ref[pl.ds(index, 1), :]
    row_ids = lax.broadcasted_iota(jnp.int32, (SPAN, SPAN), 0)
    col_ids = lax.broadcasted_iota(jnp.int32, (SPAN, SPAN), 1)
    same = ids_col == ids_row
    strict = jnp.where(same & (row_ids > col_ids), 1.0, 0.0)
    inclusive = jnp.where(same & (row_ids >= col_ids), 1.0, 0.0)
    return strict, inclusive, row_ids, col_ids


def spread(meta_ref, start, column, rows=SPAN):
    return jnp.broadcast_to(meta_ref[pl.ds(start, rows), column : column + 1], (rows, DK))


def inverse_lower(lower, row_ids, col_ids):
    size = lower.shape[0]
    step = 1
    result = jnp.where(row_ids == col_ids, 1.0, 0.0)
    while step < size:
        pair = (row_ids // (2 * step) == col_ids // (2 * step)) & (
            row_ids // step != col_ids // step
        )
        link = jnp.where(pair, lower, 0.0)
        if step == 1:
            result = result - link
        else:
            result_parts = parts_of(result)
            inner = product(parts_of(link), result_parts)
            result = result - product(result_parts, parts_of(inner))
        step = 2 * step
    return result


def mixer_forward(
    head_count,
    query_ref,
    key_ref,
    value_ref,
    gate_ref,
    logit_ref,
    taps_ref,
    gain_ref,
    meta_ref,
    ids_ref,
    mixer_ref,
    conv_ref,
    solve_ref,
    w_ref,
    u_ref,
    new_ref,
    mixed_ref,
    states_ref,
    state,
):
    state[...] = jnp.zeros_like(state)
    gain = gain_ref[...]

    def step(index, carry):
        start = pl.multiple_of(index * SPAN, SPAN)
        rows = pl.ds(start, SPAN)
        strict, inclusive, row_ids, col_ids = block_masks(meta_ref, ids_ref, start, index)
        tap_masks = [None] + [spread(meta_ref, start, lag_step) for lag_step in range(1, CONV)]
        opening = spread(meta_ref, start, 4)
        closing = spread(meta_ref, start, 5)
        carried = spread(meta_ref, start, 6)
        betas = sigmoid(logit_ref[rows, :])
        for head in range(head_count):
            columns = slice(head * DK, (head + 1) * DK)
            acts = []
            for which, ref in enumerate((query_ref, key_ref, value_ref)):
                stacked = with_earlier(ref, start, columns)
                tap = 4 * which
                total = taps_ref[tap : tap + 1, columns] * lag_rows(stacked, 0)
                for lag_step in range(1, CONV):
                    total = total + (
                        taps_ref[tap + lag_step : tap + lag_step + 1, columns]
                        * lag_rows(stacked, lag_step)
                        * tap_masks[lag_step]
                    )
                conv_ref[which, rows, columns] = total
                acts.append(total * sigmoid(total))
            unit = [
                act * lax.rsqrt(jnp.sum(act * act, axis=-1, keepdims=True) + EPS_UNIT)
                for act in acts[:2]
            ]
            queries, keys, values = unit[0].astype(LOW), unit[1].astype(LOW), acts[2].astype(LOW)
            beta = jnp.broadcast_to(betas[:, head : head + 1], (SPAN, DK))
            gram = product((keys,), (keys,), 1, 1)
            solve = inverse_lower(beta * gram * strict, row_ids, col_ids)
            solve_ref[head, rows, :] = solve
            solve_parts = parts_of(solve)
            w_rows = product(solve_parts, parts_of(beta * keys.astype(FULL)))
            u_rows = product(solve_parts, parts_of(beta * values.astype(FULL)))
            w_ref[rows, columns] = w_rows
            u_ref[rows, columns] = u_rows
            probes = product((queries,), (keys,), 1, 1) * inclusive
            before = state[head]
            states_ref[head, rows, :] = before
            before_parts = parts_of(before)
            new_value = u_rows - opening * product(parts_of(w_rows), before_parts)
            new_ref[rows, columns] = new_value
            mixed = opening * product((queries,), before_parts) + product(
                parts_of(probes), parts_of(new_value)
            )
            mixed_ref[rows, columns] = mixed
            state[head] = carried * before + product(
                (keys,), parts_of(closing * new_value), 0, 0
            )
            scale = lax.rsqrt(jnp.mean(mixed * mixed, axis=-1, keepdims=True) + EPS_HEAD)
            gates = gate_ref[rows, columns]
            mixer_ref[rows, columns] = (mixed * scale * gain * (gates * sigmoid(gates))).astype(LOW)
        return carry

    lax.fori_loop(0, query_ref.shape[0] // SPAN, step, 0)


def mixer_backward(
    head_count,
    d_mixer_ref,
    query_ref,
    key_ref,
    value_ref,
    gate_ref,
    logit_ref,
    taps_ref,
    gain_ref,
    meta_ref,
    ids_ref,
    conv_ref,
    solve_ref,
    w_ref,
    u_ref,
    new_ref,
    mixed_ref,
    states_ref,
    d_query_ref,
    d_key_ref,
    d_value_ref,
    d_gate_ref,
    d_logit_ref,
    d_taps_ref,
    d_gain_ref,
    d_state,
    later,
):
    d_state[...] = jnp.zeros_like(d_state)
    later[...] = jnp.zeros_like(later)
    d_taps_ref[...] = jnp.zeros_like(d_taps_ref)
    d_gain_ref[...] = jnp.zeros_like(d_gain_ref)
    gain = gain_ref[...]
    total_rows = query_ref.shape[0]
    count = total_rows // SPAN

    def step(back, carry):
        index = count - 1 - back
        start = pl.multiple_of(index * SPAN, SPAN)
        rows = pl.ds(start, SPAN)
        strict, inclusive, row_ids, col_ids = block_masks(meta_ref, ids_ref, start, index)
        after = pl.multiple_of(jnp.minimum(start + SPAN, total_rows - PAD), PAD)
        tap_masks = [None] + [
            jnp.concatenate(
                [
                    spread(meta_ref, start, lag_step),
                    spread(meta_ref, after, lag_step, PAD),
                ],
                axis=0,
            )
            for lag_step in range(1, CONV)
        ]
        opening = spread(meta_ref, start, 4)
        closing = spread(meta_ref, start, 5)
        carried = spread(meta_ref, start, 6)
        betas = sigmoid(logit_ref[rows, :])
        lanes = lax.broadcasted_iota(jnp.int32, (SPAN, DK), 1)
        d_logits = jnp.zeros((SPAN, DK), FULL)
        d_gain = jnp.zeros((1, DK), FULL)
        for head in range(head_count):
            columns = slice(head * DK, (head + 1) * DK)
            d_mixer = d_mixer_ref[rows, columns]
            gates = gate_ref[rows, columns]
            logistic = sigmoid(gates)
            mixed = mixed_ref[rows, columns]
            scale = lax.rsqrt(jnp.mean(mixed * mixed, axis=-1, keepdims=True) + EPS_HEAD)
            unit_mixed = mixed * scale
            d_gate_ref[rows, columns] = (
                d_mixer * (unit_mixed * gain) * (logistic * (1.0 + gates * (1.0 - logistic)))
            ).astype(LOW)
            d_normed = d_mixer * (gates * logistic)
            d_gain = d_gain + jnp.sum(d_normed * unit_mixed, axis=0, keepdims=True)
            weighted = d_normed * gain
            inner = jnp.mean(weighted * mixed, axis=-1, keepdims=True)
            d_out = scale * weighted - mixed * (scale * scale * scale) * inner
            convs = [conv_ref[which, rows, columns] for which in range(3)]
            logistics = [sigmoid(conv) for conv in convs]
            acts = [conv * logistic for conv, logistic in zip(convs, logistics)]
            scales = [
                lax.rsqrt(jnp.sum(act * act, axis=-1, keepdims=True) + EPS_UNIT)
                for act in acts[:2]
            ]
            queries = (acts[0] * scales[0]).astype(LOW)
            keys = (acts[1] * scales[1]).astype(LOW)
            values = acts[2].astype(LOW)
            beta = jnp.broadcast_to(betas[:, head : head + 1], (SPAN, DK))
            gram = product((keys,), (keys,), 1, 1)
            probes = product((queries,), (keys,), 1, 1) * inclusive
            solve_parts = parts_of(solve_ref[head, rows, :])
            w_parts = parts_of(w_ref[rows, columns])
            u_parts = parts_of(u_ref[rows, columns])
            new_value = new_ref[rows, columns]
            new_parts = parts_of(new_value)
            before_parts = parts_of(states_ref[head, rows, :])
            d_after = d_state[head]
            d_after_parts = parts_of(d_after)
            d_out_parts = parts_of(d_out)
            d_new = product(parts_of(probes), d_out_parts, 0, 0) + closing * product(
                (keys,), d_after_parts
            )
            opened_out = opening * d_out
            opened_new = opening * d_new
            d_state[head] = (
                carried * d_after
                + product((queries,), parts_of(opened_out), 0, 0)
                - product(w_parts, parts_of(opened_new), 0, 0)
            )
            d_probe = product(d_out_parts, new_parts, 1, 1) * inclusive
            d_probe_parts = parts_of(d_probe)
            d_query = product(d_probe_parts, (keys,)) + product(
                parts_of(opened_out), before_parts, 1, 1
            )
            d_key = product(d_probe_parts, (queries,), 0, 0) + closing * product(
                new_parts, d_after_parts, 1, 1
            )
            d_w = -product(parts_of(opened_new), before_parts, 1, 1)
            right_w = product(solve_parts, parts_of(d_w), 0, 0)
            right_u = product(solve_parts, parts_of(d_new), 0, 0)
            d_lower = (
                -(
                    product(parts_of(right_w), w_parts, 1, 1)
                    + product(parts_of(right_u), u_parts, 1, 1)
                )
                * strict
            )
            d_beta = jnp.sum(
                right_w * keys.astype(FULL) + right_u * values.astype(FULL) + d_lower * gram,
                axis=-1,
                keepdims=True,
            )
            beta_col = betas[:, head : head + 1]
            d_logits = d_logits + jnp.where(
                lanes == head, d_beta * beta_col * (1.0 - beta_col), 0.0
            )
            d_gram_parts = parts_of(beta * d_lower)
            d_key = (
                d_key
                + beta * right_w
                + product(d_gram_parts, (keys,))
                + product(d_gram_parts, (keys,), 0, 0)
            )
            d_value = beta * right_u
            d_acts = [
                scales[which] * grads
                - acts[which]
                * (scales[which] * scales[which] * scales[which])
                * jnp.sum(grads * acts[which], axis=-1, keepdims=True)
                for which, grads in enumerate((d_query, d_key))
            ] + [d_value]
            for which, (ref, out_ref) in enumerate(
                ((query_ref, d_query_ref), (key_ref, d_key_ref), (value_ref, d_value_ref))
            ):
                logistic = logistics[which]
                d_conv = d_acts[which] * (logistic * (1.0 + convs[which] * (1.0 - logistic)))
                tap = 4 * which
                following = jnp.concatenate([d_conv, later[which, :, columns]], axis=0)
                earlier = with_earlier(ref, start, columns)
                later[which, :, columns] = d_conv[:PAD]
                total = taps_ref[tap : tap + 1, columns] * d_conv
                d_taps = [jnp.sum(d_conv * lag_rows(earlier, 0), axis=0, keepdims=True)]
                for lag_step in range(1, CONV):
                    masked = following * tap_masks[lag_step]
                    total = total + taps_ref[
                        tap + lag_step : tap + lag_step + 1, columns
                    ] * lead_rows(masked, lag_step)
                    d_taps.append(
                        jnp.sum(
                            masked[:SPAN] * lag_rows(earlier, lag_step), axis=0, keepdims=True
                        )
                    )
                out_ref[rows, columns] = total.astype(LOW)
                for lag_step in range(CONV):
                    place = slice(tap + lag_step, tap + lag_step + 1)
                    d_taps_ref[place, columns] = d_taps_ref[place, columns] + d_taps[lag_step]
        d_logit_ref[rows, :] = d_logits.astype(LOW)
        d_gain_ref[...] = d_gain_ref[...] + d_gain
        return carry

    lax.fori_loop(0, count, step, 0)


def whole_blocks(count):
    return [pl.BlockSpec(memory_space=pltpu.VMEM)] * count


def run_mixer_forward(projections, logits, taps, gain, meta, ids):
    rows, width = projections[0].shape
    head_count = width // DK
    tall = jax.ShapeDtypeStruct((rows, width), FULL)
    square = jax.ShapeDtypeStruct((head_count, rows, DK), FULL)
    return pl.pallas_call(
        functools.partial(mixer_forward, head_count),
        out_shape=(
            jax.ShapeDtypeStruct((rows, width), LOW),
            jax.ShapeDtypeStruct((3, rows, width), FULL),
            square,
            tall,
            tall,
            tall,
            tall,
            square,
        ),
        in_specs=whole_blocks(9),
        out_specs=tuple(whole_blocks(8)),
        scratch_shapes=[pltpu.VMEM((head_count, DK, DK), FULL)],
        compiler_params=pltpu.CompilerParams(vmem_limit_bytes=56 * 1024 * 1024),
        name="mixer_forward",
    )(*projections, logits, taps, gain, meta, ids)


def run_mixer_backward(d_mixer, projections, logits, taps, gain, meta, ids, kept):
    rows, width = projections[0].shape
    head_count = width // DK
    low = jax.ShapeDtypeStruct((rows, width), LOW)
    return pl.pallas_call(
        functools.partial(mixer_backward, head_count),
        out_shape=(
            low,
            low,
            low,
            low,
            jax.ShapeDtypeStruct((rows, DK), LOW),
            jax.ShapeDtypeStruct(taps.shape, FULL),
            jax.ShapeDtypeStruct((1, DK), FULL),
        ),
        in_specs=whole_blocks(17),
        out_specs=tuple(whole_blocks(7)),
        scratch_shapes=[
            pltpu.VMEM((head_count, DK, DK), FULL),
            pltpu.VMEM((3, PAD, width), FULL),
        ],
        compiler_params=pltpu.CompilerParams(vmem_limit_bytes=56 * 1024 * 1024),
        name="mixer_backward",
    )(d_mixer, *projections, logits, taps, gain, meta, ids, *kept)


def document_tables(doc_ids):
    rows = doc_ids.shape[0]
    columns = [doc_ids.astype(FULL)]
    for lag_step in range(1, CONV):
        before = jnp.concatenate(
            [jnp.full((lag_step,), -1, jnp.int32), doc_ids[: rows - lag_step]]
        )
        columns.append((doc_ids == before).astype(FULL))
    blocks = doc_ids.reshape(rows // SPAN, SPAN)
    prior = jnp.concatenate([jnp.full((1,), -1, jnp.int32), blocks[:-1, SPAN - 1]])[:, None]
    last = blocks[:, SPAN - 1 :]
    columns.append((blocks == prior).astype(FULL).reshape(-1))
    columns.append((blocks == last).astype(FULL).reshape(-1))
    columns.append(jnp.broadcast_to(last == prior, blocks.shape).astype(FULL).reshape(-1))
    columns.append(jnp.zeros((rows,), FULL))
    return jnp.stack(columns, axis=1), blocks.astype(FULL)


def by_pairs(values, bit):
    count = lax.axis_size("mp")
    return lax.ppermute(values, "mp", [(here, here ^ bit) for here in range(count)])


def gather_rows(values):
    if lax.axis_size("mp") != 4:
        return lax.all_gather(values, "mp", axis=0, tiled=True)
    here = lax.axis_index("mp")
    other_core = by_pairs(values, 1)
    other_chip = by_pairs(values, 2)
    far = by_pairs(other_chip, 1)
    odd_core, odd_chip = here % 2 == 1, here // 2 == 1
    near_pair = jnp.where(
        odd_core,
        jnp.concatenate([other_core, values]),
        jnp.concatenate([values, other_core]),
    )
    far_pair = jnp.where(
        odd_core, jnp.concatenate([far, other_chip]), jnp.concatenate([other_chip, far])
    )
    return jnp.where(
        odd_chip, jnp.concatenate([far_pair, near_pair]), jnp.concatenate([near_pair, far_pair])
    )


def scatter_sum(values):
    if lax.axis_size("mp") != 4:
        return lax.psum_scatter(values, "mp", scatter_dimension=0, tiled=True)
    here = lax.axis_index("mp")
    core, chip = here % 2, here // 2
    quarters = values.reshape(2, 2, values.shape[0] // 4, values.shape[1])
    sent = lax.dynamic_index_in_dim(quarters, 1 - core, 1, keepdims=False).astype(LOW)
    kept = lax.dynamic_index_in_dim(quarters, core, 1, keepdims=False)
    halves = kept + by_pairs(sent, 1).astype(FULL)
    sent = lax.dynamic_index_in_dim(halves, 1 - chip, 0, keepdims=False).astype(LOW)
    kept = lax.dynamic_index_in_dim(halves, chip, 0, keepdims=False)
    return kept + by_pairs(sent, 2).astype(FULL)


def inverse_root(values, epsilon):
    return lax.rsqrt(jnp.mean(values * values, axis=-1, keepdims=True) + epsilon)


def norm_back(values, scales, gains, grads):
    weighted = grads * gains
    inner_sum = jnp.mean(weighted * values, axis=-1, keepdims=True)
    return scales * weighted - values * (scales * scales * scales) * inner_sum


def sigmoid_linear(values):
    return values * sigmoid(values)


def sigmoid_slope(values):
    logistic = sigmoid(values)
    return logistic * (1.0 + values * (1.0 - logistic))


def doc_index(lengths, length):
    starts = jnp.cumsum(lengths, axis=1) - lengths
    places = jnp.arange(length, dtype=jnp.int32)
    within = jnp.sum((starts[:, :, None] <= places[None, None, :]).astype(jnp.int32), axis=1) - 1
    offsets = jnp.arange(lengths.shape[0], dtype=jnp.int32)[:, None] * lengths.shape[1]
    return (within + offsets).reshape(-1)


def dot_full(equation, left, right):
    return jnp.einsum(equation, left, right, preferred_element_type=FULL)


def ffn_terms(rows, grad_rows, gate_weight, up_weight, down_weight):
    gate_pre = dot_full("td,df->tf", rows, gate_weight)
    up_pre = dot_full("td,df->tf", rows, up_weight)
    d_hidden = dot_full("td,fd->tf", grad_rows, down_weight)
    gate_swish = sigmoid_linear(gate_pre)
    hidden_low = (gate_swish * up_pre).astype(LOW)
    d_gate_low = (d_hidden * up_pre * sigmoid_slope(gate_pre)).astype(LOW)
    d_up_low = (d_hidden * gate_swish).astype(LOW)
    return hidden_low, d_gate_low, d_up_low


def ffn_grads(rows, grad_rows, gate_weight, up_weight, down_weight):
    hidden_low, d_gate_low, d_up_low = ffn_terms(
        rows, grad_rows, gate_weight, up_weight, down_weight
    )
    return (
        dot_full("td,tf->df", rows, d_gate_low),
        dot_full("td,tf->df", rows, d_up_low),
        dot_full("tf,td->fd", hidden_low, grad_rows),
    )


def on_device(
    inputs,
    doc_lengths,
    cotangent,
    norm_gain,
    query_weight,
    key_weight,
    value_weight,
    beta_weight,
    gating_weight,
    conv_weight,
    head_gain,
    output_weight,
    ffn_gain,
    gate_weight,
    up_weight,
    down_weight,
):
    local_rows = inputs.shape[0]
    group_rows = local_rows * lax.axis_size("mp")
    width = query_weight.shape[1]
    head_count = width // DK
    meta, ids = document_tables(doc_index(doc_lengths, group_rows // doc_lengths.shape[0]))
    taps = conv_weight.reshape(3 * CONV, width)
    gain_row = head_gain[None, :]

    everyone = group_rows * lax.axis_size("dp") <= ROWS_MOST
    if everyone:
        all_grad_rows = lax.all_gather(cotangent, ("dp", "mp"), axis=0, tiled=True)
    residual_in = inputs.astype(FULL)
    scale_one = inverse_root(residual_in, EPS_NORM)
    normed = gather_rows((residual_in * scale_one * norm_gain).astype(LOW))
    grad_rows = gather_rows(cotangent)
    weights = (query_weight, key_weight, value_weight, gating_weight)
    projections = tuple(dot_full("td,df->tf", normed, weight) for weight in weights)
    logits = dot_full("td,df->tf", normed, beta_weight)
    mixer_low, *kept = run_mixer_forward(projections, logits, taps, gain_row, meta, ids)
    attended = scatter_sum(dot_full("tf,fd->td", mixer_low, output_weight))
    residual_mid = residual_in + attended
    scale_two = inverse_root(residual_mid, EPS_NORM)
    ffn_local = (residual_mid * scale_two * ffn_gain).astype(LOW)
    ffn_input = gather_rows(ffn_local)
    if everyone:
        all_ffn_input = lax.all_gather(ffn_local, ("dp", "mp"), axis=0, tiled=True)

    hidden_low, d_gate_low, d_up_low = ffn_terms(
        ffn_input, grad_rows, gate_weight, up_weight, down_weight
    )
    d_ffn_norm = scatter_sum(
        dot_full("tf,df->td", d_gate_low, gate_weight) + dot_full("tf,df->td", d_up_low, up_weight)
    )
    ffn_out = scatter_sum(dot_full("tf,fd->td", hidden_low, down_weight))
    output = (residual_mid + ffn_out).astype(LOW)
    d_ffn = None
    if not everyone:
        d_ffn = (
            dot_full("td,tf->df", ffn_input, d_gate_low),
            dot_full("td,tf->df", ffn_input, d_up_low),
            dot_full("tf,td->fd", hidden_low, grad_rows),
        )

    d_mid = cotangent.astype(FULL) + norm_back(residual_mid, scale_two, ffn_gain, d_ffn_norm)
    ffn_gain_part = jnp.sum(d_ffn_norm * residual_mid * scale_two, axis=0)
    mid_rows = gather_rows(d_mid.astype(LOW))
    d_output_w = dot_full("tf,td->fd", mixer_low, mid_rows)
    d_mixer = dot_full("td,fd->tf", mid_rows, output_weight)
    *low_grads, d_logits, d_taps, head_gain_part = run_mixer_backward(
        d_mixer, projections, logits, taps, gain_row, meta, ids, kept
    )
    d_logits = d_logits[:, :head_count]
    summed = dot_full("tf,df->td", d_logits, beta_weight)
    for grads, weight in zip(low_grads, weights):
        summed = summed + dot_full("tf,df->td", grads, weight)
    d_normed = scatter_sum(summed)
    input_grad = d_mid + norm_back(residual_in, scale_one, norm_gain, d_normed)
    norm_gain_part = jnp.sum(d_normed * residual_in * scale_one, axis=0)
    proj_grads = [dot_full("td,tf->df", normed, grads).astype(LOW) for grads in low_grads]
    d_beta_w = dot_full("td,tf->df", normed, d_logits)

    gains = jnp.concatenate([norm_gain_part, ffn_gain_part, head_gain_part[0]])
    gains = lax.psum(gains, "mp")
    small = jnp.concatenate([d_beta_w.reshape(-1), d_taps.reshape(-1), gains])
    size = small.shape[0]
    padded = -(-size // (16 * 512)) * 16 * 512
    small = jnp.pad(small, (0, padded - size)).reshape(-1, 512).astype(LOW)
    if everyone:
        d_ffn = ffn_grads(all_ffn_input, all_grad_rows, gate_weight, up_weight, down_weight)
    else:
        d_ffn = [grads.astype(FULL) for grads in lax.psum([d.astype(LOW) for d in d_ffn], "dp")]
    d_gate_w, d_up_w, d_down = d_ffn
    *proj_grads, d_output_w, small = [
        grads.astype(FULL)
        for grads in lax.psum(proj_grads + [d_output_w.astype(LOW), small], "dp")
    ]
    small = small.reshape(-1)
    beta_size, taps_size = d_beta_w.size, taps.size
    d_beta_w = small[:beta_size].reshape(d_beta_w.shape)
    d_conv = small[beta_size : beta_size + taps_size].reshape(conv_weight.shape)
    gains = small[beta_size + taps_size : size]
    features = inputs.shape[1]
    return (
        output,
        input_grad,
        gains[:features],
        proj_grads[0],
        proj_grads[1],
        proj_grads[2],
        d_beta_w,
        proj_grads[3],
        d_conv,
        gains[2 * features :],
        d_output_w,
        gains[features : 2 * features],
        d_gate_w,
        d_up_w,
        d_down,
    )


def solution(mesh):
    rows, columns = P(("dp", "mp"), None), P(None, "mp")
    return jax.shard_map(
        on_device,
        mesh=mesh,
        in_specs=(
            rows,
            P("dp", None),
            rows,
            P(),
            columns,
            columns,
            columns,
            columns,
            columns,
            P(None, None, "mp"),
            P(),
            P("mp", None),
            P(),
            columns,
            columns,
            P("mp", None),
        ),
        out_specs=(
            rows,
            rows,
            P(),
            columns,
            columns,
            columns,
            columns,
            columns,
            P(None, None, "mp"),
            P(),
            P("mp", None),
            P(),
            columns,
            columns,
            P("mp", None),
        ),
        check_vma=False,
    )
```

```python
import functools

import jax
import jax.numpy as jnp
from jax import lax
from jax.experimental import pallas as pl
from jax.experimental.pallas import tpu as pltpu
from jax.sharding import PartitionSpec as P

DK = 128
CONV = 4
SPAN = 128
PAD = 8
ROWS_MOST = 8192


EPS_NORM = 1e-06
EPS_UNIT = 1e-06
EPS_HEAD = 0.05
LOW = jnp.bfloat16
FULL = jnp.float32


def sigmoid(values):
    return 1.0 / (1.0 + jnp.exp(-values))


def parts_of(values):
    high = values.astype(LOW)
    return (high, (values - high.astype(FULL)).astype(LOW))


def product(left, right, left_dim=1, right_dim=0):
    dims = (((left_dim,), (right_dim,)), ((), ()))
    right_free = 1 - right_dim
    width = right[0].shape[right_free]
    if len(left) == 2:
        left_all = jnp.concatenate(left, axis=left_dim)
        first = jnp.concatenate([right[0], right[0]], axis=right_dim)
    else:
        left_all, first = left[0], right[0]
    if len(right) == 1:
        return lax.dot_general(left_all, first, dims, preferred_element_type=FULL)
    second = right[1]
    if len(left) == 2:
        second = jnp.concatenate([second, jnp.zeros_like(second)], axis=right_dim)
    both = lax.dot_general(
        left_all,
        jnp.concatenate([first, second], axis=right_free),
        dims,
        preferred_element_type=FULL,
    )
    return both[:, :width] + both[:, width:]


def lag_rows(stacked, lag_step):
    if lag_step == 0:
        return stacked[PAD:]
    return pltpu.roll(stacked, lag_step, axis=0)[PAD:]


def lead_rows(stacked, lag_step):
    rows = stacked.shape[0]
    if lag_step == 0:
        return stacked[: rows - PAD]
    return pltpu.roll(stacked, rows - lag_step, axis=0)[: rows - PAD]


def with_earlier(ref, start, columns):
    before = pl.multiple_of(jnp.maximum(start - PAD, 0), PAD)
    return jnp.concatenate(
        [ref[pl.ds(before, PAD), columns], ref[pl.ds(start, SPAN), columns]], axis=0
    )


def block_masks(meta_ref, ids_ref, start, index):
    ids_col = meta_ref[pl.ds(start, SPAN), 0:1]
    ids_row = ids_ref[pl.ds(index, 1), :]
    row_ids = lax.broadcasted_iota(jnp.int32, (SPAN, SPAN), 0)
    col_ids = lax.broadcasted_iota(jnp.int32, (SPAN, SPAN), 1)
    same = ids_col == ids_row
    strict = jnp.where(same & (row_ids > col_ids), 1.0, 0.0)
    inclusive = jnp.where(same & (row_ids >= col_ids), 1.0, 0.0)
    return strict, inclusive, row_ids, col_ids


def spread(meta_ref, start, column, rows=SPAN):
    return jnp.broadcast_to(meta_ref[pl.ds(start, rows), column : column + 1], (rows, DK))


def inverse_lower(lower, row_ids, col_ids):
    size = lower.shape[0]
    step = 1
    result = jnp.where(row_ids == col_ids, 1.0, 0.0)
    while step < size:
        pair = (row_ids // (2 * step) == col_ids // (2 * step)) & (
            row_ids // step != col_ids // step
        )
        link = jnp.where(pair, lower, 0.0)
        if step == 1:
            result = result - link
        else:
            result_parts = parts_of(result)
            inner = product(parts_of(link), result_parts)
            result = result - product(result_parts, parts_of(inner))
        step = 2 * step
    return result


def mixer_forward(
    head_count,
    query_ref,
    key_ref,
    value_ref,
    gate_ref,
    logit_ref,
    taps_ref,
    gain_ref,
    meta_ref,
    ids_ref,
    mixer_ref,
    conv_ref,
    solve_ref,
    w_ref,
    u_ref,
    new_ref,
    mixed_ref,
    states_ref,
    state,
):
    state[...] = jnp.zeros_like(state)
    gain = gain_ref[...]

    def step(index, carry):
        start = pl.multiple_of(index * SPAN, SPAN)
        rows = pl.ds(start, SPAN)
        strict, inclusive, row_ids, col_ids = block_masks(meta_ref, ids_ref, start, index)
        tap_masks = [None] + [spread(meta_ref, start, lag_step) for lag_step in range(1, CONV)]
        opening = spread(meta_ref, start, 4)
        closing = spread(meta_ref, start, 5)
        carried = spread(meta_ref, start, 6)
        betas = sigmoid(logit_ref[rows, :])
        for head in range(head_count):
            columns = slice(head * DK, (head + 1) * DK)
            acts = []
            for which, ref in enumerate((query_ref, key_ref, value_ref)):
                stacked = with_earlier(ref, start, columns)
                tap = 4 * which
                total = taps_ref[tap : tap + 1, columns] * lag_rows(stacked, 0)
                for lag_step in range(1, CONV):
                    total = total + (
                        taps_ref[tap + lag_step : tap + lag_step + 1, columns]
                        * lag_rows(stacked, lag_step)
                        * tap_masks[lag_step]
                    )
                conv_ref[which, rows, columns] = total
                acts.append(total * sigmoid(total))
            unit = [
                act * lax.rsqrt(jnp.sum(act * act, axis=-1, keepdims=True) + EPS_UNIT)
                for act in acts[:2]
            ]
            queries, keys, values = unit[0].astype(LOW), unit[1].astype(LOW), acts[2].astype(LOW)
            beta = jnp.broadcast_to(betas[:, head : head + 1], (SPAN, DK))
            gram = product((keys,), (keys,), 1, 1)
            solve = inverse_lower(beta * gram * strict, row_ids, col_ids)
            solve_ref[head, rows, :] = solve
            solve_parts = parts_of(solve)
            w_rows = product(solve_parts, parts_of(beta * keys.astype(FULL)))
            u_rows = product(solve_parts, parts_of(beta * values.astype(FULL)))
            w_ref[rows, columns] = w_rows
            u_ref[rows, columns] = u_rows
            probes = product((queries,), (keys,), 1, 1) * inclusive
            before = state[head]
            states_ref[head, rows, :] = before
            before_parts = parts_of(before)
            new_value = u_rows - opening * product(parts_of(w_rows), before_parts)
            new_ref[rows, columns] = new_value
            mixed = opening * product((queries,), before_parts) + product(
                parts_of(probes), parts_of(new_value)
            )
            mixed_ref[rows, columns] = mixed
            state[head] = carried * before + product(
                (keys,), parts_of(closing * new_value), 0, 0
            )
            scale = lax.rsqrt(jnp.mean(mixed * mixed, axis=-1, keepdims=True) + EPS_HEAD)
            gates = gate_ref[rows, columns]
            mixer_ref[rows, columns] = (mixed * scale * gain * (gates * sigmoid(gates))).astype(LOW)
        return carry

    lax.fori_loop(0, query_ref.shape[0] // SPAN, step, 0)


def mixer_backward(
    head_count,
    d_mixer_ref,
    query_ref,
    key_ref,
    value_ref,
    gate_ref,
    logit_ref,
    taps_ref,
    gain_ref,
    meta_ref,
    ids_ref,
    conv_ref,
    solve_ref,
    w_ref,
    u_ref,
    new_ref,
    mixed_ref,
    states_ref,
    d_query_ref,
    d_key_ref,
    d_value_ref,
    d_logit_ref,
    d_taps_ref,
    d_gain_ref,
    d_state,
    later,
):
    d_state[...] = jnp.zeros_like(d_state)
    later[...] = jnp.zeros_like(later)
    d_taps_ref[...] = jnp.zeros_like(d_taps_ref)
    d_gain_ref[...] = jnp.zeros_like(d_gain_ref)
    gain = gain_ref[...]
    total_rows = query_ref.shape[0]
    count = total_rows // SPAN

    def step(back, carry):
        index = count - 1 - back
        start = pl.multiple_of(index * SPAN, SPAN)
        rows = pl.ds(start, SPAN)
        strict, inclusive, row_ids, col_ids = block_masks(meta_ref, ids_ref, start, index)
        after = pl.multiple_of(jnp.minimum(start + SPAN, total_rows - PAD), PAD)
        tap_masks = [None] + [
            jnp.concatenate(
                [
                    spread(meta_ref, start, lag_step),
                    spread(meta_ref, after, lag_step, PAD),
                ],
                axis=0,
            )
            for lag_step in range(1, CONV)
        ]
        opening = spread(meta_ref, start, 4)
        closing = spread(meta_ref, start, 5)
        carried = spread(meta_ref, start, 6)
        betas = sigmoid(logit_ref[rows, :])
        lanes = lax.broadcasted_iota(jnp.int32, (SPAN, DK), 1)
        d_logits = jnp.zeros((SPAN, DK), FULL)
        d_gain = jnp.zeros((1, DK), FULL)
        for head in range(head_count):
            columns = slice(head * DK, (head + 1) * DK)
            d_mixer = d_mixer_ref[rows, columns]
            gates = gate_ref[rows, columns]
            logistic = sigmoid(gates)
            mixed = mixed_ref[rows, columns]
            scale = lax.rsqrt(jnp.mean(mixed * mixed, axis=-1, keepdims=True) + EPS_HEAD)
            unit_mixed = mixed * scale
            d_normed = d_mixer * (gates * logistic)
            d_gain = d_gain + jnp.sum(d_normed * unit_mixed, axis=0, keepdims=True)
            weighted = d_normed * gain
            inner = jnp.mean(weighted * mixed, axis=-1, keepdims=True)
            d_out = scale * weighted - mixed * (scale * scale * scale) * inner
            convs = [conv_ref[which, rows, columns] for which in range(3)]
            logistics = [sigmoid(conv) for conv in convs]
            acts = [conv * logistic for conv, logistic in zip(convs, logistics)]
            scales = [
                lax.rsqrt(jnp.sum(act * act, axis=-1, keepdims=True) + EPS_UNIT)
                for act in acts[:2]
            ]
            queries = (acts[0] * scales[0]).astype(LOW)
            keys = (acts[1] * scales[1]).astype(LOW)
            values = acts[2].astype(LOW)
            beta = jnp.broadcast_to(betas[:, head : head + 1], (SPAN, DK))
            gram = product((keys,), (keys,), 1, 1)
            probes = product((queries,), (keys,), 1, 1) * inclusive
            solve_parts = parts_of(solve_ref[head, rows, :])
            w_parts = parts_of(w_ref[rows, columns])
            u_parts = parts_of(u_ref[rows, columns])
            new_value = new_ref[rows, columns]
            new_parts = parts_of(new_value)
            before_parts = parts_of(states_ref[head, rows, :])
            d_after = d_state[head]
            d_after_parts = parts_of(d_after)
            d_out_parts = parts_of(d_out)
            d_new = product(parts_of(probes), d_out_parts, 0, 0) + closing * product(
                (keys,), d_after_parts
            )
            opened_out = opening * d_out
            opened_new = opening * d_new
            d_state[head] = (
                carried * d_after
                + product((queries,), parts_of(opened_out), 0, 0)
                - product(w_parts, parts_of(opened_new), 0, 0)
            )
            d_probe = product(d_out_parts, new_parts, 1, 1) * inclusive
            d_probe_parts = parts_of(d_probe)
            d_query = product(d_probe_parts, (keys,)) + product(
                parts_of(opened_out), before_parts, 1, 1
            )
            d_key = product(d_probe_parts, (queries,), 0, 0) + closing * product(
                new_parts, d_after_parts, 1, 1
            )
            d_w = -product(parts_of(opened_new), before_parts, 1, 1)
            right_w = product(solve_parts, parts_of(d_w), 0, 0)
            right_u = product(solve_parts, parts_of(d_new), 0, 0)
            d_lower = (
                -(
                    product(parts_of(right_w), w_parts, 1, 1)
                    + product(parts_of(right_u), u_parts, 1, 1)
                )
                * strict
            )
            d_beta = jnp.sum(
                right_w * keys.astype(FULL) + right_u * values.astype(FULL) + d_lower * gram,
                axis=-1,
                keepdims=True,
            )
            beta_col = betas[:, head : head + 1]
            d_logits = d_logits + jnp.where(
                lanes == head, d_beta * beta_col * (1.0 - beta_col), 0.0
            )
            d_gram_parts = parts_of(beta * d_lower)
            d_key = (
                d_key
                + beta * right_w
                + product(d_gram_parts, (keys,))
                + product(d_gram_parts, (keys,), 0, 0)
            )
            d_value = beta * right_u
            d_acts = [
                scales[which] * grads
                - acts[which]
                * (scales[which] * scales[which] * scales[which])
                * jnp.sum(grads * acts[which], axis=-1, keepdims=True)
                for which, grads in enumerate((d_query, d_key))
            ] + [d_value]
            for which, (ref, out_ref) in enumerate(
                ((query_ref, d_query_ref), (key_ref, d_key_ref), (value_ref, d_value_ref))
            ):
                logistic = logistics[which]
                d_conv = d_acts[which] * (logistic * (1.0 + convs[which] * (1.0 - logistic)))
                tap = 4 * which
                following = jnp.concatenate([d_conv, later[which, :, columns]], axis=0)
                earlier = with_earlier(ref, start, columns)
                later[which, :, columns] = d_conv[:PAD]
                total = taps_ref[tap : tap + 1, columns] * d_conv
                d_taps = [jnp.sum(d_conv * lag_rows(earlier, 0), axis=0, keepdims=True)]
                for lag_step in range(1, CONV):
                    masked = following * tap_masks[lag_step]
                    total = total + taps_ref[
                        tap + lag_step : tap + lag_step + 1, columns
                    ] * lead_rows(masked, lag_step)
                    d_taps.append(
                        jnp.sum(
                            masked[:SPAN] * lag_rows(earlier, lag_step), axis=0, keepdims=True
                        )
                    )
                out_ref[rows, columns] = total.astype(LOW)
                for lag_step in range(CONV):
                    place = slice(tap + lag_step, tap + lag_step + 1)
                    d_taps_ref[place, columns] = d_taps_ref[place, columns] + d_taps[lag_step]
        d_logit_ref[rows, :] = d_logits.astype(LOW)
        d_gain_ref[...] = d_gain_ref[...] + d_gain
        return carry

    lax.fori_loop(0, count, step, 0)


def whole_blocks(count):
    return [pl.BlockSpec(memory_space=pltpu.VMEM)] * count


def run_mixer_forward(projections, logits, taps, gain, meta, ids):
    rows, width = projections[0].shape
    head_count = width // DK
    tall = jax.ShapeDtypeStruct((rows, width), FULL)
    square = jax.ShapeDtypeStruct((head_count, rows, DK), FULL)
    return pl.pallas_call(
        functools.partial(mixer_forward, head_count),
        out_shape=(
            jax.ShapeDtypeStruct((rows, width), LOW),
            jax.ShapeDtypeStruct((3, rows, width), FULL),
            square,
            tall,
            tall,
            tall,
            tall,
            square,
        ),
        in_specs=whole_blocks(9),
        out_specs=tuple(whole_blocks(8)),
        scratch_shapes=[pltpu.VMEM((head_count, DK, DK), FULL)],
        compiler_params=pltpu.CompilerParams(vmem_limit_bytes=56 * 1024 * 1024),
        name="mixer_forward",
    )(*projections, logits, taps, gain, meta, ids)


def run_mixer_backward(d_mixer, projections, logits, taps, gain, meta, ids, kept):
    rows, width = projections[0].shape
    head_count = width // DK
    low = jax.ShapeDtypeStruct((rows, width), LOW)
    return pl.pallas_call(
        functools.partial(mixer_backward, head_count),
        out_shape=(
            low,
            low,
            low,
            jax.ShapeDtypeStruct((rows, DK), LOW),
            jax.ShapeDtypeStruct(taps.shape, FULL),
            jax.ShapeDtypeStruct((1, DK), FULL),
        ),
        in_specs=whole_blocks(17),
        out_specs=tuple(whole_blocks(6)),
        scratch_shapes=[
            pltpu.VMEM((head_count, DK, DK), FULL),
            pltpu.VMEM((3, PAD, width), FULL),
        ],
        compiler_params=pltpu.CompilerParams(vmem_limit_bytes=56 * 1024 * 1024),
        name="mixer_backward",
    )(d_mixer, *projections, logits, taps, gain, meta, ids, *kept)


def document_tables(doc_ids):
    rows = doc_ids.shape[0]
    columns = [doc_ids.astype(FULL)]
    for lag_step in range(1, CONV):
        before = jnp.concatenate(
            [jnp.full((lag_step,), -1, jnp.int32), doc_ids[: rows - lag_step]]
        )
        columns.append((doc_ids == before).astype(FULL))
    blocks = doc_ids.reshape(rows // SPAN, SPAN)
    prior = jnp.concatenate([jnp.full((1,), -1, jnp.int32), blocks[:-1, SPAN - 1]])[:, None]
    last = blocks[:, SPAN - 1 :]
    columns.append((blocks == prior).astype(FULL).reshape(-1))
    columns.append((blocks == last).astype(FULL).reshape(-1))
    columns.append(jnp.broadcast_to(last == prior, blocks.shape).astype(FULL).reshape(-1))
    columns.append(jnp.zeros((rows,), FULL))
    return jnp.stack(columns, axis=1), blocks.astype(FULL)


def mm(left, right, left_dim, right_dim):
    return lax.dot_general(
        left, right, (((left_dim,), (right_dim,)), ((), ())), preferred_element_type=FULL
    )


FFN_TILE = 128
FFN_ROWS = 1024
TICKS = 8
X_SENT, X_GOT, OWN, IN_SENT, IN_GOT, MID_SENT, MID_GOT, OUT_SENT, OUT_GOT, BACK_SENT, BACK_GOT, KEPT = range(12)


def add_into(target_ref, other_ref):
    rows = target_ref.shape[0]
    piece = min(rows, 128)

    def add(index, carry):
        place = pl.ds(pl.multiple_of(index * piece, piece), piece)
        target_ref[place, :] = (
            target_ref[place, :].astype(FULL) + other_ref[place, :].astype(FULL)
        ).astype(LOW)
        return carry

    lax.fori_loop(0, rows // piece, add, 0)


def ffn_step(rows_ref, grads_ref, gate_ref, up_ref, down_ref, d_gate_ref, d_up_ref, d_down_ref, total):
    block, tile = pl.program_id(1), gate_ref.shape[1]

    @pl.when(block == 0)
    def _():
        total[...] = jnp.zeros_like(total)

    rows, grads = rows_ref[...], grads_ref[...]
    both = mm(rows, jnp.concatenate([gate_ref[...], up_ref[...]], axis=1), 1, 0)
    gate_pre, up_pre = both[:, :tile], both[:, tile:]
    d_hidden = mm(grads, down_ref[...], 1, 1)
    logistic = sigmoid(gate_pre)
    gate_swish = gate_pre * logistic
    hidden_low = (gate_swish * up_pre).astype(LOW)
    d_gate_low = (d_hidden * up_pre * (logistic * (1.0 + gate_pre * (1.0 - logistic)))).astype(LOW)
    d_up_low = (d_hidden * gate_swish).astype(LOW)
    total[: 2 * tile] += mm(jnp.concatenate([d_gate_low, d_up_low], axis=1), rows, 0, 0)
    total[2 * tile :] += mm(hidden_low, grads, 0, 0)

    @pl.when(block == pl.num_programs(1) - 1)
    def _():
        d_gate_ref[...] = total[:tile].T.astype(LOW)
        d_up_ref[...] = total[tile : 2 * tile].T.astype(LOW)
        d_down_ref[...] = total[2 * tile :].astype(LOW)


def ffn_and_sums(orders, ticks, *refs):
    count = len(orders)
    ffn_refs, given = refs[:5], refs[5 : 5 + count]
    d_refs, made = refs[5 + count : 8 + count], refs[8 + count : 8 + 2 * count]
    scratch = refs[8 + 2 * count :]
    total, sems = scratch[0], scratch[1]
    halves, owns, ins, mids = (
        scratch[2 + kind * count : 2 + (kind + 1) * count] for kind in range(4)
    )
    step = pl.program_id(0) * pl.num_programs(1) + pl.program_id(1)
    here = lax.axis_index("dp")
    side, place = here % 2, here // 2
    pair = here + 1 - 2 * side
    near = 2 * (place + 1 - 2 * (place % 2)) + side
    far = 2 * (3 - place) + side
    middle = (place == 1) | (place == 2)
    end = (place == 0) | (place == 3)

    @pl.when(step == 0)
    def _():
        barrier = pltpu.get_barrier_semaphore()
        pl.semaphore_signal(barrier, inc=1, device_id={"dp": pair})
        pl.semaphore_signal(barrier, inc=1, device_id={"dp": near})

        @pl.when(middle)
        def _():
            pl.semaphore_signal(barrier, inc=1, device_id={"dp": far})
            pl.semaphore_wait(barrier, 3)

        @pl.when(end)
        def _():
            pl.semaphore_wait(barrier, 2)

    def plan(which):
        rows = halves[which].shape[0]
        mine = pl.ds(pl.multiple_of(side * rows, rows), rows)
        theirs = pl.ds(pl.multiple_of((1 - side) * rows, rows), rows)

        def remote(source, target, sent, got, device):
            return pltpu.make_async_remote_copy(
                src_ref=source,
                dst_ref=target,
                send_sem=sems.at[which, sent],
                recv_sem=sems.at[which, got],
                device_id={"dp": device},
            )

        def local(source, target, sem):
            return pltpu.make_async_copy(source, target, sems.at[which, sem])

        return dict(
            across=lambda: remote(given[which].at[theirs], halves[which], X_SENT, X_GOT, pair),
            own=lambda: local(given[which].at[mine], owns[which], OWN),
            inward=lambda: remote(halves[which], ins[which], IN_SENT, IN_GOT, near),
            middle=lambda: remote(halves[which], mids[which], MID_SENT, MID_GOT, far),
            outward=lambda: remote(halves[which], made[which].at[mine], OUT_SENT, OUT_GOT, near),
            back_end=lambda: remote(made[which].at[mine], made[which].at[mine], BACK_SENT, BACK_GOT, pair),
            back_middle=lambda: remote(halves[which], made[which].at[mine], BACK_SENT, BACK_GOT, pair),
            back_got=lambda: remote(made[which].at[theirs], made[which].at[theirs], BACK_SENT, BACK_GOT, pair),
            kept=lambda: local(halves[which], made[which].at[mine], KEPT),
        )

    def stage(which, number):
        copies = plan(which)
        if number == 0:
            copies["across"]().start()
            copies["own"]().start()
        elif number == 1:
            copies["own"]().wait()
            copies["across"]().wait()
            add_into(halves[which], owns[which])

            @pl.when(end)
            def _():
                copies["inward"]().start()
        elif number == 2:

            @pl.when(end)
            def _():
                copies["inward"]().wait_send()

            @pl.when(middle)
            def _():
                copies["inward"]().wait_recv()
                add_into(halves[which], ins[which])
                copies["middle"]().start()
        elif number == 3:

            @pl.when(middle)
            def _():
                copies["middle"]().wait()
                add_into(halves[which], mids[which])
                copies["outward"]().start()
                copies["back_middle"]().start()
                copies["kept"]().start()
        elif number == 4:

            @pl.when(end)
            def _():
                copies["outward"]().wait_recv()
                copies["back_end"]().start()

            @pl.when(middle)
            def _():
                copies["outward"]().wait_send()
                copies["kept"]().wait()
        else:

            @pl.when(end)
            def _():
                copies["back_end"]().wait_send()

            @pl.when(middle)
            def _():
                copies["back_middle"]().wait_send()
            copies["back_got"]().wait_recv()

    for tick in range(TICKS):

        @pl.when(step == ticks[tick])
        def _(tick=tick):
            for which, order in reversed(list(enumerate(orders))):
                if 0 <= tick - order <= 5:
                    stage(which, tick - order)

    ffn_step(*ffn_refs, *d_refs, total)


def run_ffn_and_sums(rows, grads, gate_weight, up_weight, down_weight, given, orders):
    total_rows, features = rows.shape
    units = gate_weight.shape[1]
    block_rows = min(FFN_ROWS, total_rows)
    blocks, tiles = total_rows // block_rows, units // FFN_TILE
    steps = blocks * tiles
    ticks = [((steps - 1) * tick) // (TICKS - 1) for tick in range(TICKS)]
    across = pl.BlockSpec((features, FFN_TILE), lambda tile, block: (0, tile))
    down = pl.BlockSpec((FFN_TILE, features), lambda tile, block: (tile, 0))
    tall = pl.BlockSpec((block_rows, features), lambda tile, block: (block, 0))
    anywhere = [pl.BlockSpec(memory_space=pl.ANY)] * len(given)
    half_shapes = [(values.shape[0] // 2, values.shape[1]) for values in given]
    return pl.pallas_call(
        functools.partial(ffn_and_sums, orders, ticks),
        grid=(tiles, blocks),
        in_specs=[tall, tall, across, across, down] + anywhere,
        out_specs=[across, across, down] + anywhere,
        out_shape=[
            jax.ShapeDtypeStruct((features, units), LOW),
            jax.ShapeDtypeStruct((features, units), LOW),
            jax.ShapeDtypeStruct((units, features), LOW),
        ]
        + [jax.ShapeDtypeStruct(values.shape, LOW) for values in given],
        scratch_shapes=[
            pltpu.VMEM((3 * FFN_TILE, features), FULL),
            pltpu.SemaphoreType.DMA((len(given), 12)),
        ]
        + [pltpu.VMEM(shape, LOW) for kind in range(4) for shape in half_shapes],
        compiler_params=pltpu.CompilerParams(
            vmem_limit_bytes=60 * 1024 * 1024, collective_id=0, has_side_effects=True
        ),
        cost_estimate=pl.CostEstimate(
            flops=12 * total_rows * features * units,
            bytes_accessed=4 * tiles * total_rows * features,
            transcendentals=total_rows * units,
        ),
        name="ffn_and_sums",
    )(rows, grads, gate_weight, up_weight, down_weight, *given)


def by_pairs(values, bit):
    count = lax.axis_size("mp")
    return lax.ppermute(values, "mp", [(here, here ^ bit) for here in range(count)])


def gather_rows(values):
    if lax.axis_size("mp") != 4:
        return lax.all_gather(values, "mp", axis=0, tiled=True)
    here = lax.axis_index("mp")
    other_core = by_pairs(values, 1)
    other_chip = by_pairs(values, 2)
    far = by_pairs(other_chip, 1)
    odd_core, odd_chip = here % 2 == 1, here // 2 == 1
    near_pair = jnp.where(
        odd_core,
        jnp.concatenate([other_core, values]),
        jnp.concatenate([values, other_core]),
    )
    far_pair = jnp.where(
        odd_core, jnp.concatenate([far, other_chip]), jnp.concatenate([other_chip, far])
    )
    return jnp.where(
        odd_chip, jnp.concatenate([far_pair, near_pair]), jnp.concatenate([near_pair, far_pair])
    )


def scatter_sum(values):
    if lax.axis_size("mp") != 4:
        return lax.psum_scatter(values, "mp", scatter_dimension=0, tiled=True)
    here = lax.axis_index("mp")
    core, chip = here % 2, here // 2
    quarters = values.reshape(2, 2, values.shape[0] // 4, values.shape[1])
    sent = lax.dynamic_index_in_dim(quarters, 1 - core, 1, keepdims=False).astype(LOW)
    kept = lax.dynamic_index_in_dim(quarters, core, 1, keepdims=False)
    halves = kept + by_pairs(sent, 1).astype(FULL)
    sent = lax.dynamic_index_in_dim(halves, 1 - chip, 0, keepdims=False).astype(LOW)
    kept = lax.dynamic_index_in_dim(halves, chip, 0, keepdims=False)
    return kept + by_pairs(sent, 2).astype(FULL)


def inverse_root(values, epsilon):
    return lax.rsqrt(jnp.mean(values * values, axis=-1, keepdims=True) + epsilon)


def norm_back(values, scales, gains, grads):
    weighted = grads * gains
    inner_sum = jnp.mean(weighted * values, axis=-1, keepdims=True)
    return scales * weighted - values * (scales * scales * scales) * inner_sum


def sigmoid_linear(values):
    return values * sigmoid(values)


def sigmoid_slope(values):
    logistic = sigmoid(values)
    return logistic * (1.0 + values * (1.0 - logistic))


def gate_back(d_mixer, mixed, gates, head_gain):
    shape = mixed.shape
    heads = mixed.reshape(shape[0], shape[1] // DK, DK)
    normed = (heads * inverse_root(heads, EPS_HEAD) * head_gain).reshape(shape)
    return (d_mixer * normed * sigmoid_slope(gates)).astype(LOW)


def doc_index(lengths, length):
    starts = jnp.cumsum(lengths, axis=1) - lengths
    places = jnp.arange(length, dtype=jnp.int32)
    within = jnp.sum((starts[:, :, None] <= places[None, None, :]).astype(jnp.int32), axis=1) - 1
    offsets = jnp.arange(lengths.shape[0], dtype=jnp.int32)[:, None] * lengths.shape[1]
    return (within + offsets).reshape(-1)


def dot_full(equation, left, right):
    return jnp.einsum(equation, left, right, preferred_element_type=FULL)


def ffn_terms(rows, grad_rows, gate_weight, up_weight, down_weight):
    gate_pre = dot_full("td,df->tf", rows, gate_weight)
    up_pre = dot_full("td,df->tf", rows, up_weight)
    d_hidden = dot_full("td,fd->tf", grad_rows, down_weight)
    gate_swish = sigmoid_linear(gate_pre)
    hidden_low = (gate_swish * up_pre).astype(LOW)
    d_gate_low = (d_hidden * up_pre * sigmoid_slope(gate_pre)).astype(LOW)
    d_up_low = (d_hidden * gate_swish).astype(LOW)
    return hidden_low, d_gate_low, d_up_low


def on_device(
    inputs,
    doc_lengths,
    cotangent,
    norm_gain,
    query_weight,
    key_weight,
    value_weight,
    beta_weight,
    gating_weight,
    conv_weight,
    head_gain,
    output_weight,
    ffn_gain,
    gate_weight,
    up_weight,
    down_weight,
):
    local_rows = inputs.shape[0]
    group_rows = local_rows * lax.axis_size("mp")
    width = query_weight.shape[1]
    head_count = width // DK
    meta, ids = document_tables(doc_index(doc_lengths, group_rows // doc_lengths.shape[0]))
    taps = conv_weight.reshape(3 * CONV, width)
    gain_row = head_gain[None, :]

    everyone = group_rows * lax.axis_size("dp") <= ROWS_MOST and lax.axis_size("dp") == 8
    if everyone:
        all_grad_rows = lax.all_gather(cotangent, ("dp", "mp"), axis=0, tiled=True)
    residual_in = inputs.astype(FULL)
    scale_one = inverse_root(residual_in, EPS_NORM)
    normed = gather_rows((residual_in * scale_one * norm_gain).astype(LOW))
    weights = (query_weight, key_weight, value_weight, gating_weight)
    projections = tuple(dot_full("td,df->tf", normed, weight) for weight in weights)
    logits = dot_full("td,df->tf", normed, beta_weight)
    mixer_low, *kept = run_mixer_forward(projections, logits, taps, gain_row, meta, ids)
    attended = scatter_sum(dot_full("tf,fd->td", mixer_low, output_weight))
    residual_mid = residual_in + attended
    scale_two = inverse_root(residual_mid, EPS_NORM)
    ffn_local = (residual_mid * scale_two * ffn_gain).astype(LOW)
    ffn_input = gather_rows(ffn_local)
    if everyone:
        ffn_input, all_grad_rows = lax.optimization_barrier((ffn_input, all_grad_rows))
        all_ffn_input = lax.all_gather(ffn_local, ("dp", "mp"), axis=0, tiled=True)
        grad_rows = lax.dynamic_slice_in_dim(
            all_grad_rows, lax.axis_index("dp") * group_rows, group_rows, 0
        )
    else:
        grad_rows = gather_rows(cotangent)

    hidden_low, d_gate_low, d_up_low = ffn_terms(
        ffn_input, grad_rows, gate_weight, up_weight, down_weight
    )
    d_ffn_norm = scatter_sum(
        dot_full("tf,df->td", d_gate_low, gate_weight) + dot_full("tf,df->td", d_up_low, up_weight)
    )
    d_ffn = None
    if not everyone:
        d_ffn = (
            dot_full("td,tf->df", ffn_input, d_gate_low),
            dot_full("td,tf->df", ffn_input, d_up_low),
            dot_full("tf,td->fd", hidden_low, grad_rows),
        )

    d_mid = cotangent.astype(FULL) + norm_back(residual_mid, scale_two, ffn_gain, d_ffn_norm)
    ffn_gain_part = jnp.sum(d_ffn_norm * residual_mid * scale_two, axis=0)
    mid_rows = gather_rows(d_mid.astype(LOW))
    d_mixer = dot_full("td,fd->tf", mid_rows, output_weight)
    d_gate_low = gate_back(d_mixer, kept[5], projections[3], head_gain)
    early = [
        dot_full("tf,td->fd", mixer_low, mid_rows).astype(LOW),
        dot_full("td,tf->df", normed, d_gate_low).astype(LOW),
    ]
    d_mixer, *early = lax.optimization_barrier((d_mixer, *early))
    early = lax.psum(early, "dp")
    *low_grads, d_logits, d_taps, head_gain_part = run_mixer_backward(
        d_mixer, projections, logits, taps, gain_row, meta, ids, kept
    )
    d_logits = d_logits[:, :head_count]
    summed = dot_full("tf,df->td", d_logits, beta_weight)
    for grads, weight in zip(low_grads + [d_gate_low], weights):
        summed = summed + dot_full("tf,df->td", grads, weight)
    summed, hidden_low = lax.optimization_barrier((summed, hidden_low))
    d_normed = scatter_sum(summed)
    ffn_out = scatter_sum(dot_full("tf,fd->td", hidden_low, down_weight))
    output = (residual_mid + ffn_out).astype(LOW)
    input_grad = d_mid + norm_back(residual_in, scale_one, norm_gain, d_normed)
    norm_gain_part = jnp.sum(d_normed * residual_in * scale_one, axis=0)
    late = [dot_full("td,tf->df", normed, grads).astype(LOW) for grads in low_grads]
    d_beta_w = dot_full("td,tf->df", normed, d_logits)

    gains = jnp.concatenate([norm_gain_part, ffn_gain_part, head_gain_part[0]])
    if lax.axis_size("mp") == 4:
        for bit in (1, 2):
            gains = gains + by_pairs(gains, bit)
    else:
        gains = lax.psum(gains, "mp")
    small = jnp.concatenate([d_beta_w.reshape(-1), d_taps.reshape(-1), gains])
    size = small.shape[0]
    padded = -(-size // (32 * 512)) * 32 * 512
    small = jnp.pad(small, (0, padded - size)).reshape(-1, 512).astype(LOW)
    late.append(small)
    if everyone:
        *d_ffn, d_query_w, d_key_w, d_value_w, small = run_ffn_and_sums(
            all_ffn_input, all_grad_rows, gate_weight, up_weight, down_weight, late, (0, 1, 2, 2)
        )
    else:
        d_query_w, d_key_w, d_value_w, small = lax.psum(late, "dp")
        d_ffn = lax.psum([grads.astype(LOW) for grads in d_ffn], "dp")
    d_gate_w, d_up_w, d_down = [grads.astype(FULL) for grads in d_ffn]
    proj_grads = [
        grads.astype(FULL) for grads in (d_query_w, d_key_w, d_value_w, early[1])
    ]
    d_output_w = early[0].astype(FULL)
    small = small.astype(FULL)
    small = small.reshape(-1)
    beta_size, taps_size = d_beta_w.size, taps.size
    d_beta_w = small[:beta_size].reshape(d_beta_w.shape)
    d_conv = small[beta_size : beta_size + taps_size].reshape(conv_weight.shape)
    gains = small[beta_size + taps_size : size]
    features = inputs.shape[1]
    return (
        output,
        input_grad,
        gains[:features],
        proj_grads[0],
        proj_grads[1],
        proj_grads[2],
        d_beta_w,
        proj_grads[3],
        d_conv,
        gains[2 * features :],
        d_output_w,
        gains[features : 2 * features],
        d_gate_w,
        d_up_w,
        d_down,
    )


def solution(mesh):
    rows, columns = P(("dp", "mp"), None), P(None, "mp")
    return jax.shard_map(
        on_device,
        mesh=mesh,
        in_specs=(
            rows,
            P("dp", None),
            rows,
            P(),
            columns,
            columns,
            columns,
            columns,
            columns,
            P(None, None, "mp"),
            P(),
            P("mp", None),
            P(),
            columns,
            columns,
            P("mp", None),
        ),
        out_specs=(
            rows,
            rows,
            P(),
            columns,
            columns,
            columns,
            columns,
            columns,
            P(None, None, "mp"),
            P(),
            P("mp", None),
            P(),
            columns,
            columns,
            P("mp", None),
        ),
        check_vma=False,
    )
```

```python
import functools
import math

import jax
import jax.numpy as jnp
from jax import lax
from jax.experimental import pallas as pl
from jax.experimental.pallas import tpu as pltpu
from jax.sharding import PartitionSpec as P

DK = 128
CONV = 4
SPAN = 128
PAD = 8
ROWS_MOST = 8192


EPS_NORM = 1e-06
EPS_UNIT = 1e-06
EPS_HEAD = 0.05
LOW = jnp.bfloat16
FULL = jnp.float32


def sigmoid(values):
    return 1.0 / (1.0 + jnp.exp(-values))


def parts_of(values):
    high = values.astype(LOW)
    return (high, (values - high.astype(FULL)).astype(LOW))


def product(left, right, left_dim=1, right_dim=0):
    dims = (((left_dim,), (right_dim,)), ((), ()))
    right_free = 1 - right_dim
    width = right[0].shape[right_free]
    if len(left) == 2:
        left_all = jnp.concatenate(left, axis=left_dim)
        first = jnp.concatenate([right[0], right[0]], axis=right_dim)
    else:
        left_all, first = left[0], right[0]
    if len(right) == 1:
        return lax.dot_general(left_all, first, dims, preferred_element_type=FULL)
    second = right[1]
    if len(left) == 2:
        second = jnp.concatenate([second, jnp.zeros_like(second)], axis=right_dim)
    both = lax.dot_general(
        left_all,
        jnp.concatenate([first, second], axis=right_free),
        dims,
        preferred_element_type=FULL,
    )
    return both[:, :width] + both[:, width:]


def lag_rows(stacked, lag_step):
    if lag_step == 0:
        return stacked[PAD:]
    return pltpu.roll(stacked, lag_step, axis=0)[PAD:]


def lead_rows(stacked, lag_step):
    rows = stacked.shape[0]
    if lag_step == 0:
        return stacked[: rows - PAD]
    return pltpu.roll(stacked, rows - lag_step, axis=0)[: rows - PAD]


def with_earlier(ref, start, columns):
    before = pl.multiple_of(jnp.maximum(start - PAD, 0), PAD)
    return jnp.concatenate(
        [ref[pl.ds(before, PAD), columns], ref[pl.ds(start, SPAN), columns]], axis=0
    )


def block_masks(meta_ref, ids_ref, start, index):
    ids_col = meta_ref[pl.ds(start, SPAN), 0:1]
    ids_row = ids_ref[pl.ds(index, 1), :]
    row_ids = lax.broadcasted_iota(jnp.int32, (SPAN, SPAN), 0)
    col_ids = lax.broadcasted_iota(jnp.int32, (SPAN, SPAN), 1)
    same = ids_col == ids_row
    strict = jnp.where(same & (row_ids > col_ids), 1.0, 0.0)
    inclusive = jnp.where(same & (row_ids >= col_ids), 1.0, 0.0)
    return strict, inclusive, row_ids, col_ids


def spread(meta_ref, start, column, rows=SPAN):
    return jnp.broadcast_to(meta_ref[pl.ds(start, rows), column : column + 1], (rows, DK))


def inverse_lower(lower, row_ids, col_ids):
    size = lower.shape[0]
    step = 1
    result = jnp.where(row_ids == col_ids, 1.0, 0.0)
    while step < size:
        pair = (row_ids // (2 * step) == col_ids // (2 * step)) & (
            row_ids // step != col_ids // step
        )
        link = jnp.where(pair, lower, 0.0)
        if step == 1:
            result = result - link
        else:
            result_parts = parts_of(result)
            inner = product(parts_of(link), result_parts)
            yield
            result = result - product(result_parts, parts_of(inner))
            yield
        step = 2 * step
    return result


def side_by_side(works):
    works = list(works)
    while works:
        left = []
        for work in works:
            try:
                next(work)
                left.append(work)
            except StopIteration:
                pass
        works = left


def mixer_forward(
    head_count,
    query_ref,
    key_ref,
    value_ref,
    gate_ref,
    logit_ref,
    taps_ref,
    gain_ref,
    meta_ref,
    ids_ref,
    mixer_ref,
    conv_ref,
    solve_ref,
    w_ref,
    u_ref,
    new_ref,
    mixed_ref,
    states_ref,
    state,
):
    state[...] = jnp.zeros_like(state)
    gain = gain_ref[...]

    def step(index, carry):
        start = pl.multiple_of(index * SPAN, SPAN)
        rows = pl.ds(start, SPAN)
        strict, inclusive, row_ids, col_ids = block_masks(meta_ref, ids_ref, start, index)
        tap_masks = [None] + [spread(meta_ref, start, lag_step) for lag_step in range(1, CONV)]
        opening = spread(meta_ref, start, 4)
        closing = spread(meta_ref, start, 5)
        carried = spread(meta_ref, start, 6)
        betas = sigmoid(logit_ref[rows, :])
        def work(head):
            columns = slice(head * DK, (head + 1) * DK)
            acts = []
            for which, ref in enumerate((query_ref, key_ref, value_ref)):
                stacked = with_earlier(ref, start, columns)
                tap = 4 * which
                total = taps_ref[tap : tap + 1, columns] * lag_rows(stacked, 0)
                for lag_step in range(1, CONV):
                    total = total + (
                        taps_ref[tap + lag_step : tap + lag_step + 1, columns]
                        * lag_rows(stacked, lag_step)
                        * tap_masks[lag_step]
                    )
                conv_ref[which, rows, columns] = total
                acts.append(total * sigmoid(total))
            unit = [
                act * lax.rsqrt(jnp.sum(act * act, axis=-1, keepdims=True) + EPS_UNIT)
                for act in acts[:2]
            ]
            queries, keys, values = unit[0].astype(LOW), unit[1].astype(LOW), acts[2].astype(LOW)
            yield
            beta = jnp.broadcast_to(betas[:, head : head + 1], (SPAN, DK))
            gram = product((keys,), (keys,), 1, 1)
            yield
            solve = yield from inverse_lower(beta * gram * strict, row_ids, col_ids)
            solve_ref[head, rows, :] = solve
            solve_parts = parts_of(solve)
            w_rows = product(solve_parts, parts_of(beta * keys.astype(FULL)))
            u_rows = product(solve_parts, parts_of(beta * values.astype(FULL)))
            w_ref[rows, columns] = w_rows
            u_ref[rows, columns] = u_rows
            yield
            probes = product((queries,), (keys,), 1, 1) * inclusive
            before = state[head]
            states_ref[head, rows, :] = before
            before_parts = parts_of(before)
            new_value = u_rows - opening * product(parts_of(w_rows), before_parts)
            new_ref[rows, columns] = new_value
            yield
            mixed = opening * product((queries,), before_parts) + product(
                parts_of(probes), parts_of(new_value)
            )
            mixed_ref[rows, columns] = mixed
            yield
            state[head] = carried * before + product(
                (keys,), parts_of(closing * new_value), 0, 0
            )
            scale = lax.rsqrt(jnp.mean(mixed * mixed, axis=-1, keepdims=True) + EPS_HEAD)
            gates = gate_ref[rows, columns]
            mixer_ref[rows, columns] = (mixed * scale * gain * (gates * sigmoid(gates))).astype(LOW)

        side_by_side(work(head) for head in range(head_count))
        return carry

    lax.fori_loop(0, query_ref.shape[0] // SPAN, step, 0)


def mixer_backward(
    head_count,
    d_mixer_ref,
    query_ref,
    key_ref,
    value_ref,
    gate_ref,
    logit_ref,
    taps_ref,
    gain_ref,
    meta_ref,
    ids_ref,
    conv_ref,
    solve_ref,
    w_ref,
    u_ref,
    new_ref,
    mixed_ref,
    states_ref,
    d_query_ref,
    d_key_ref,
    d_value_ref,
    d_logit_ref,
    d_taps_ref,
    d_gain_ref,
    d_state,
    later,
):
    d_state[...] = jnp.zeros_like(d_state)
    later[...] = jnp.zeros_like(later)
    d_taps_ref[...] = jnp.zeros_like(d_taps_ref)
    d_gain_ref[...] = jnp.zeros_like(d_gain_ref)
    gain = gain_ref[...]
    total_rows = query_ref.shape[0]
    count = total_rows // SPAN

    def step(back, carry):
        index = count - 1 - back
        start = pl.multiple_of(index * SPAN, SPAN)
        rows = pl.ds(start, SPAN)
        strict, inclusive, row_ids, col_ids = block_masks(meta_ref, ids_ref, start, index)
        after = pl.multiple_of(jnp.minimum(start + SPAN, total_rows - PAD), PAD)
        tap_masks = [None] + [
            jnp.concatenate(
                [
                    spread(meta_ref, start, lag_step),
                    spread(meta_ref, after, lag_step, PAD),
                ],
                axis=0,
            )
            for lag_step in range(1, CONV)
        ]
        opening = spread(meta_ref, start, 4)
        closing = spread(meta_ref, start, 5)
        carried = spread(meta_ref, start, 6)
        betas = sigmoid(logit_ref[rows, :])
        lanes = lax.broadcasted_iota(jnp.int32, (SPAN, DK), 1)
        d_logits = jnp.zeros((SPAN, DK), FULL)
        d_gain = jnp.zeros((1, DK), FULL)
        def work(head):
            nonlocal d_gain, d_logits
            columns = slice(head * DK, (head + 1) * DK)
            d_mixer = d_mixer_ref[rows, columns]
            gates = gate_ref[rows, columns]
            logistic = sigmoid(gates)
            mixed = mixed_ref[rows, columns]
            scale = lax.rsqrt(jnp.mean(mixed * mixed, axis=-1, keepdims=True) + EPS_HEAD)
            unit_mixed = mixed * scale
            d_normed = d_mixer * (gates * logistic)
            d_gain = d_gain + jnp.sum(d_normed * unit_mixed, axis=0, keepdims=True)
            weighted = d_normed * gain
            inner = jnp.mean(weighted * mixed, axis=-1, keepdims=True)
            d_out = scale * weighted - mixed * (scale * scale * scale) * inner
            yield
            convs = [conv_ref[which, rows, columns] for which in range(3)]
            logistics = [sigmoid(conv) for conv in convs]
            acts = [conv * logistic for conv, logistic in zip(convs, logistics)]
            scales = [
                lax.rsqrt(jnp.sum(act * act, axis=-1, keepdims=True) + EPS_UNIT)
                for act in acts[:2]
            ]
            queries = (acts[0] * scales[0]).astype(LOW)
            keys = (acts[1] * scales[1]).astype(LOW)
            values = acts[2].astype(LOW)
            beta = jnp.broadcast_to(betas[:, head : head + 1], (SPAN, DK))
            gram = product((keys,), (keys,), 1, 1)
            probes = product((queries,), (keys,), 1, 1) * inclusive
            solve_parts = parts_of(solve_ref[head, rows, :])
            w_parts = parts_of(w_ref[rows, columns])
            u_parts = parts_of(u_ref[rows, columns])
            new_value = new_ref[rows, columns]
            new_parts = parts_of(new_value)
            before_parts = parts_of(states_ref[head, rows, :])
            yield
            d_after = d_state[head]
            d_after_parts = parts_of(d_after)
            d_out_parts = parts_of(d_out)
            d_new = product(parts_of(probes), d_out_parts, 0, 0) + closing * product(
                (keys,), d_after_parts
            )
            yield
            opened_out = opening * d_out
            opened_new = opening * d_new
            d_state[head] = (
                carried * d_after
                + product((queries,), parts_of(opened_out), 0, 0)
                - product(w_parts, parts_of(opened_new), 0, 0)
            )
            yield
            d_probe = product(d_out_parts, new_parts, 1, 1) * inclusive
            d_probe_parts = parts_of(d_probe)
            yield
            d_query = product(d_probe_parts, (keys,)) + product(
                parts_of(opened_out), before_parts, 1, 1
            )
            yield
            d_key = product(d_probe_parts, (queries,), 0, 0) + closing * product(
                new_parts, d_after_parts, 1, 1
            )
            yield
            d_w = -product(parts_of(opened_new), before_parts, 1, 1)
            yield
            right_w = product(solve_parts, parts_of(d_w), 0, 0)
            right_u = product(solve_parts, parts_of(d_new), 0, 0)
            yield
            d_lower = (
                -(
                    product(parts_of(right_w), w_parts, 1, 1)
                    + product(parts_of(right_u), u_parts, 1, 1)
                )
                * strict
            )
            yield
            d_beta = jnp.sum(
                right_w * keys.astype(FULL) + right_u * values.astype(FULL) + d_lower * gram,
                axis=-1,
                keepdims=True,
            )
            beta_col = betas[:, head : head + 1]
            d_logits = d_logits + jnp.where(
                lanes == head, d_beta * beta_col * (1.0 - beta_col), 0.0
            )
            yield
            d_gram_parts = parts_of(beta * d_lower)
            d_key = (
                d_key
                + beta * right_w
                + product(d_gram_parts, (keys,))
                + product(d_gram_parts, (keys,), 0, 0)
            )
            yield
            d_value = beta * right_u
            yield
            d_acts = [
                scales[which] * grads
                - acts[which]
                * (scales[which] * scales[which] * scales[which])
                * jnp.sum(grads * acts[which], axis=-1, keepdims=True)
                for which, grads in enumerate((d_query, d_key))
            ] + [d_value]
            for which, (ref, out_ref) in enumerate(
                ((query_ref, d_query_ref), (key_ref, d_key_ref), (value_ref, d_value_ref))
            ):
                logistic = logistics[which]
                d_conv = d_acts[which] * (logistic * (1.0 + convs[which] * (1.0 - logistic)))
                tap = 4 * which
                following = jnp.concatenate([d_conv, later[which, :, columns]], axis=0)
                earlier = with_earlier(ref, start, columns)
                later[which, :, columns] = d_conv[:PAD]
                total = taps_ref[tap : tap + 1, columns] * d_conv
                d_taps = [jnp.sum(d_conv * lag_rows(earlier, 0), axis=0, keepdims=True)]
                for lag_step in range(1, CONV):
                    masked = following * tap_masks[lag_step]
                    total = total + taps_ref[
                        tap + lag_step : tap + lag_step + 1, columns
                    ] * lead_rows(masked, lag_step)
                    d_taps.append(
                        jnp.sum(
                            masked[:SPAN] * lag_rows(earlier, lag_step), axis=0, keepdims=True
                        )
                    )
                out_ref[rows, columns] = total.astype(LOW)
                for lag_step in range(CONV):
                    place = slice(tap + lag_step, tap + lag_step + 1)
                    d_taps_ref[place, columns] = d_taps_ref[place, columns] + d_taps[lag_step]

        side_by_side(work(head) for head in range(head_count))
        d_logit_ref[rows, :] = d_logits.astype(LOW)
        d_gain_ref[...] = d_gain_ref[...] + d_gain
        return carry

    lax.fori_loop(0, count, step, 0)


def whole_blocks(count):
    return [pl.BlockSpec(memory_space=pltpu.VMEM)] * count


def run_mixer_forward(projections, logits, taps, gain, meta, ids):
    rows, width = projections[0].shape
    head_count = width // DK
    tall = jax.ShapeDtypeStruct((rows, width), FULL)
    square = jax.ShapeDtypeStruct((head_count, rows, DK), FULL)
    return pl.pallas_call(
        functools.partial(mixer_forward, head_count),
        out_shape=(
            jax.ShapeDtypeStruct((rows, width), LOW),
            jax.ShapeDtypeStruct((3, rows, width), FULL),
            square,
            tall,
            tall,
            tall,
            tall,
            square,
        ),
        in_specs=whole_blocks(9),
        out_specs=tuple(whole_blocks(8)),
        scratch_shapes=[pltpu.VMEM((head_count, DK, DK), FULL)],
        compiler_params=pltpu.CompilerParams(vmem_limit_bytes=56 * 1024 * 1024),
        name="mixer_forward",
    )(*projections, logits, taps, gain, meta, ids)


def run_mixer_backward(d_mixer, projections, logits, taps, gain, meta, ids, kept):
    rows, width = projections[0].shape
    head_count = width // DK
    low = jax.ShapeDtypeStruct((rows, width), LOW)
    return pl.pallas_call(
        functools.partial(mixer_backward, head_count),
        out_shape=(
            low,
            low,
            low,
            jax.ShapeDtypeStruct((rows, DK), LOW),
            jax.ShapeDtypeStruct(taps.shape, FULL),
            jax.ShapeDtypeStruct((1, DK), FULL),
        ),
        in_specs=whole_blocks(17),
        out_specs=tuple(whole_blocks(6)),
        scratch_shapes=[
            pltpu.VMEM((head_count, DK, DK), FULL),
            pltpu.VMEM((3, PAD, width), FULL),
        ],
        compiler_params=pltpu.CompilerParams(vmem_limit_bytes=56 * 1024 * 1024),
        name="mixer_backward",
    )(d_mixer, *projections, logits, taps, gain, meta, ids, *kept)


def document_tables(doc_ids):
    rows = doc_ids.shape[0]
    columns = [doc_ids.astype(FULL)]
    for lag_step in range(1, CONV):
        before = jnp.concatenate(
            [jnp.full((lag_step,), -1, jnp.int32), doc_ids[: rows - lag_step]]
        )
        columns.append((doc_ids == before).astype(FULL))
    blocks = doc_ids.reshape(rows // SPAN, SPAN)
    prior = jnp.concatenate([jnp.full((1,), -1, jnp.int32), blocks[:-1, SPAN - 1]])[:, None]
    last = blocks[:, SPAN - 1 :]
    columns.append((blocks == prior).astype(FULL).reshape(-1))
    columns.append((blocks == last).astype(FULL).reshape(-1))
    columns.append(jnp.broadcast_to(last == prior, blocks.shape).astype(FULL).reshape(-1))
    columns.append(jnp.zeros((rows,), FULL))
    return jnp.stack(columns, axis=1), blocks.astype(FULL)


def mm(left, right, left_dim, right_dim):
    return lax.dot_general(
        left, right, (((left_dim,), (right_dim,)), ((), ())), preferred_element_type=FULL
    )


FFN_TILE = 128
FFN_ROWS = 1024
TICKS = 9
X_SENT, X_GOT, OWN, IN_SENT, IN_GOT, MID_SENT, MID_GOT, OUT_SENT, OUT_GOT, BACK_SENT, BACK_GOT, KEPT = range(12)


def add_into(target_ref, other_ref):
    rows = target_ref.shape[0]
    piece = min(rows, 128)

    def add(index, carry):
        place = pl.ds(pl.multiple_of(index * piece, piece), piece)
        target_ref[place, :] = (
            target_ref[place, :].astype(FULL) + other_ref[place, :].astype(FULL)
        ).astype(LOW)
        return carry

    lax.fori_loop(0, rows // piece, add, 0)


def ffn_step(rows_ref, grads_ref, gate_ref, up_ref, down_ref, d_gate_ref, d_up_ref, d_down_ref, total):
    block, tile = pl.program_id(1), gate_ref.shape[1]

    @pl.when(block == 0)
    def _():
        total[...] = jnp.zeros_like(total)

    rows, grads = rows_ref[...], grads_ref[...]
    both = mm(rows, jnp.concatenate([gate_ref[...], up_ref[...]], axis=1), 1, 0)
    gate_pre, up_pre = both[:, :tile], both[:, tile:]
    d_hidden = mm(grads, down_ref[...], 1, 1)
    logistic = sigmoid(gate_pre)
    gate_swish = gate_pre * logistic
    hidden_low = (gate_swish * up_pre).astype(LOW)
    d_gate_low = (d_hidden * up_pre * (logistic * (1.0 + gate_pre * (1.0 - logistic)))).astype(LOW)
    d_up_low = (d_hidden * gate_swish).astype(LOW)
    total[: 2 * tile] += mm(jnp.concatenate([d_gate_low, d_up_low], axis=1), rows, 0, 0)
    total[2 * tile :] += mm(hidden_low, grads, 0, 0)

    @pl.when(block == pl.num_programs(1) - 1)
    def _():
        d_gate_ref[...] = total[:tile].T.astype(LOW)
        d_up_ref[...] = total[tile : 2 * tile].T.astype(LOW)
        d_down_ref[...] = total[2 * tile :].astype(LOW)


def ffn_and_sums(plans, ticks, *refs):
    count = len(plans)
    ffn_refs, given = refs[:5], refs[5 : 5 + count]
    d_refs, made = refs[5 + count : 8 + count], refs[8 + count : 8 + 2 * count]
    scratch = refs[8 + 2 * count :]
    total, sems = scratch[0], scratch[1]
    halves, owns, ins, mids = (
        scratch[2 + kind * count : 2 + (kind + 1) * count] for kind in range(4)
    )
    step = pl.program_id(0) * pl.num_programs(1) + pl.program_id(1)
    here = lax.axis_index("dp")
    side, place = here % 2, here // 2
    pair = here + 1 - 2 * side
    near = 2 * (place + 1 - 2 * (place % 2)) + side
    far = 2 * (3 - place) + side
    middle = (place == 1) | (place == 2)
    end = (place == 0) | (place == 3)

    @pl.when(step == 0)
    def _():
        barrier = pltpu.get_barrier_semaphore()
        pl.semaphore_signal(barrier, inc=1, device_id={"dp": pair})
        pl.semaphore_signal(barrier, inc=1, device_id={"dp": near})

        @pl.when(middle)
        def _():
            pl.semaphore_signal(barrier, inc=1, device_id={"dp": far})
            pl.semaphore_wait(barrier, 3)

        @pl.when(end)
        def _():
            pl.semaphore_wait(barrier, 2)

    def plan(which):
        rows = halves[which].shape[0]
        mine = pl.ds(pl.multiple_of(side * rows, rows), rows)
        theirs = pl.ds(pl.multiple_of((1 - side) * rows, rows), rows)

        def remote(source, target, sent, got, device):
            return pltpu.make_async_remote_copy(
                src_ref=source,
                dst_ref=target,
                send_sem=sems.at[which, sent],
                recv_sem=sems.at[which, got],
                device_id={"dp": device},
            )

        def local(source, target, sem):
            return pltpu.make_async_copy(source, target, sems.at[which, sem])

        return dict(
            across=lambda: remote(given[which].at[theirs], halves[which], X_SENT, X_GOT, pair),
            own=lambda: local(given[which].at[mine], owns[which], OWN),
            whole=lambda: local(given[which], halves[which], OWN),
            inward=lambda: remote(halves[which], ins[which], IN_SENT, IN_GOT, near),
            middle=lambda: remote(halves[which], mids[which], MID_SENT, MID_GOT, far),
            outward=lambda: remote(halves[which], made[which].at[mine], OUT_SENT, OUT_GOT, near),
            back_end=lambda: remote(made[which].at[mine], made[which].at[mine], BACK_SENT, BACK_GOT, pair),
            back_middle=lambda: remote(halves[which], made[which].at[mine], BACK_SENT, BACK_GOT, pair),
            back_got=lambda: remote(made[which].at[theirs], made[which].at[theirs], BACK_SENT, BACK_GOT, pair),
            kept=lambda: local(halves[which], made[which].at[mine], KEPT),
        )

    def stage(which, number):
        copies = plan(which)
        if number == 0:
            copies["across"]().start()
            copies["own"]().start()
        elif number == 1:
            if plans[which][0] is None:
                copies["whole"]().start()
                copies["whole"]().wait()
            else:
                copies["own"]().wait()
                copies["across"]().wait()
                add_into(halves[which], owns[which])

            @pl.when(end)
            def _():
                copies["inward"]().start()
        elif number == 2:

            @pl.when(end)
            def _():
                copies["inward"]().wait_send()

            @pl.when(middle)
            def _():
                copies["inward"]().wait_recv()
                add_into(halves[which], ins[which])
                copies["middle"]().start()
        elif number == 3:

            @pl.when(middle)
            def _():
                copies["middle"]().wait()
                add_into(halves[which], mids[which])
                copies["outward"]().start()
                copies["back_middle"]().start()
                copies["kept"]().start()
        elif number == 4:

            @pl.when(end)
            def _():
                copies["outward"]().wait_recv()
                copies["back_end"]().start()

            @pl.when(middle)
            def _():
                copies["outward"]().wait_send()
                copies["kept"]().wait()
        else:

            @pl.when(end)
            def _():
                copies["back_end"]().wait_send()

            @pl.when(middle)
            def _():
                copies["back_middle"]().wait_send()
            copies["back_got"]().wait_recv()

    for tick in range(TICKS):

        @pl.when(step == ticks[tick])
        def _(tick=tick):
            for which, places in enumerate(plans):
                if tick in places:
                    stage(which, places.index(tick))

    ffn_step(*ffn_refs, *d_refs, total)


def run_ffn_and_sums(rows, grads, gate_weight, up_weight, down_weight, given, plans):
    total_rows, features = rows.shape
    units = gate_weight.shape[1]
    block_rows = min(FFN_ROWS, total_rows)
    blocks, tiles = total_rows // block_rows, units // FFN_TILE
    steps = blocks * tiles
    ticks = [((steps - 1) * tick) // (TICKS - 1) for tick in range(TICKS)]
    across = pl.BlockSpec((features, FFN_TILE), lambda tile, block: (0, tile))
    down = pl.BlockSpec((FFN_TILE, features), lambda tile, block: (tile, 0))
    tall = pl.BlockSpec((block_rows, features), lambda tile, block: (block, 0))
    anywhere = [pl.BlockSpec(memory_space=pl.ANY)] * len(given)
    half_shapes = [
        values.shape if places[0] is None else (values.shape[0] // 2, values.shape[1])
        for values, places in zip(given, plans)
    ]
    own_shapes = [
        (16, 128) if places[0] is None else shape for shape, places in zip(half_shapes, plans)
    ]
    return pl.pallas_call(
        functools.partial(ffn_and_sums, plans, ticks),
        grid=(tiles, blocks),
        in_specs=[tall, tall, across, across, down] + anywhere,
        out_specs=[across, across, down] + anywhere,
        out_shape=[
            jax.ShapeDtypeStruct((features, units), LOW),
            jax.ShapeDtypeStruct((features, units), LOW),
            jax.ShapeDtypeStruct((units, features), LOW),
        ]
        + [jax.ShapeDtypeStruct((2 * rows, width), LOW) for rows, width in half_shapes],
        scratch_shapes=[
            pltpu.VMEM((3 * FFN_TILE, features), FULL),
            pltpu.SemaphoreType.DMA((len(given), 12)),
        ]
        + [
            pltpu.VMEM(shape, LOW)
            for shape in half_shapes + own_shapes + half_shapes + half_shapes
        ],
        compiler_params=pltpu.CompilerParams(
            vmem_limit_bytes=60 * 1024 * 1024, collective_id=0, has_side_effects=True
        ),
        cost_estimate=pl.CostEstimate(
            flops=12 * total_rows * features * units,
            bytes_accessed=4 * tiles * total_rows * features,
            transcendentals=total_rows * units,
        ),
        name="ffn_and_sums",
    )(rows, grads, gate_weight, up_weight, down_weight, *given)


CHIP_AXES = ("y", "core")


def swapped(values, name):
    return lax.ppermute(values, name, [(0, 1), (1, 0)])


def gather_rows(values, mp_axes):
    if mp_axes != CHIP_AXES:
        return lax.all_gather(values, mp_axes, axis=0, tiled=True)
    other_core = swapped(values, "core")
    other_chip = swapped(values, "y")
    far = swapped(other_chip, "core")
    odd_core, odd_chip = lax.axis_index("core") == 1, lax.axis_index("y") == 1
    near_pair = jnp.where(
        odd_core,
        jnp.concatenate([other_core, values]),
        jnp.concatenate([values, other_core]),
    )
    far_pair = jnp.where(
        odd_core, jnp.concatenate([far, other_chip]), jnp.concatenate([other_chip, far])
    )
    return jnp.where(
        odd_chip, jnp.concatenate([far_pair, near_pair]), jnp.concatenate([near_pair, far_pair])
    )


def scatter_near(values):
    core, chip = lax.axis_index("core"), lax.axis_index("y")
    quarters = values.reshape(2, 2, values.shape[0] // 4, values.shape[1])
    sent = lax.dynamic_index_in_dim(quarters, 1 - core, 1, keepdims=False).astype(LOW)
    kept = lax.dynamic_index_in_dim(quarters, core, 1, keepdims=False)
    halves = kept + swapped(sent, "core").astype(FULL)
    sent = lax.dynamic_index_in_dim(halves, 1 - chip, 0, keepdims=False).astype(LOW)
    return lax.dynamic_index_in_dim(halves, chip, 0, keepdims=False), sent


def scatter_sum(values, mp_axes):
    if mp_axes != CHIP_AXES:
        return lax.psum_scatter(values, mp_axes, scatter_dimension=0, tiled=True)
    kept, sent = scatter_near(values)
    return kept + swapped(sent, "y").astype(FULL)


def half_of(values, which):
    size = values.shape[0] // 2
    return lax.dynamic_slice_in_dim(values, which * size, size, 0)


def pair_sum(values):
    side = lax.axis_index("dp") % 2
    sent = lax.ppermute(half_of(values, 1 - side), "dp", [(here, here ^ 1) for here in range(8)])
    return (half_of(values, side).astype(FULL) + sent.astype(FULL)).astype(LOW)


def inverse_root(values, epsilon):
    return lax.rsqrt(jnp.mean(values * values, axis=-1, keepdims=True) + epsilon)


def norm_back(values, scales, gains, grads):
    weighted = grads * gains
    inner_sum = jnp.mean(weighted * values, axis=-1, keepdims=True)
    return scales * weighted - values * (scales * scales * scales) * inner_sum


def sigmoid_linear(values):
    return values * sigmoid(values)


def sigmoid_slope(values):
    logistic = sigmoid(values)
    return logistic * (1.0 + values * (1.0 - logistic))


def gate_back(d_mixer, mixed, gates, head_gain):
    shape = mixed.shape
    heads = mixed.reshape(shape[0], shape[1] // DK, DK)
    normed = (heads * inverse_root(heads, EPS_HEAD) * head_gain).reshape(shape)
    return (d_mixer * normed * sigmoid_slope(gates)).astype(LOW)


def doc_index(lengths, length):
    starts = jnp.cumsum(lengths, axis=1) - lengths
    places = jnp.arange(length, dtype=jnp.int32)
    within = jnp.sum((starts[:, :, None] <= places[None, None, :]).astype(jnp.int32), axis=1) - 1
    offsets = jnp.arange(lengths.shape[0], dtype=jnp.int32)[:, None] * lengths.shape[1]
    return (within + offsets).reshape(-1)


def dot_full(equation, left, right):
    return jnp.einsum(equation, left, right, preferred_element_type=FULL)


def ffn_terms(rows, grad_rows, gate_weight, up_weight, down_weight):
    gate_pre = dot_full("td,df->tf", rows, gate_weight)
    up_pre = dot_full("td,df->tf", rows, up_weight)
    d_hidden = dot_full("td,fd->tf", grad_rows, down_weight)
    gate_swish = sigmoid_linear(gate_pre)
    hidden_low = (gate_swish * up_pre).astype(LOW)
    d_gate_low = (d_hidden * up_pre * sigmoid_slope(gate_pre)).astype(LOW)
    d_up_low = (d_hidden * gate_swish).astype(LOW)
    return hidden_low, d_gate_low, d_up_low


def on_device(
    mp_axes,
    inputs,
    doc_lengths,
    cotangent,
    norm_gain,
    query_weight,
    key_weight,
    value_weight,
    beta_weight,
    gating_weight,
    conv_weight,
    head_gain,
    output_weight,
    ffn_gain,
    gate_weight,
    up_weight,
    down_weight,
):
    local_rows = inputs.shape[0]
    group_rows = local_rows * math.prod(lax.axis_size(name) for name in mp_axes)
    width = query_weight.shape[1]
    head_count = width // DK
    meta, ids = document_tables(doc_index(doc_lengths, group_rows // doc_lengths.shape[0]))
    taps = conv_weight.reshape(3 * CONV, width)
    gain_row = head_gain[None, :]

    everyone = (
        mp_axes == CHIP_AXES
        and lax.axis_size("dp") == 8
        and group_rows * lax.axis_size("dp") <= ROWS_MOST
    )
    if everyone:
        all_grad_rows = lax.all_gather(cotangent, ("dp", *mp_axes), axis=0, tiled=True)
    residual_in = inputs.astype(FULL)
    scale_one = inverse_root(residual_in, EPS_NORM)
    normed = gather_rows((residual_in * scale_one * norm_gain).astype(LOW), mp_axes)
    weights = (query_weight, key_weight, value_weight, gating_weight)
    projections = tuple(dot_full("td,df->tf", normed, weight) for weight in weights)
    logits = dot_full("td,df->tf", normed, beta_weight)
    mixer_low, *kept = run_mixer_forward(projections, logits, taps, gain_row, meta, ids)
    attended = scatter_sum(dot_full("tf,fd->td", mixer_low, output_weight), mp_axes)
    residual_mid = residual_in + attended
    scale_two = inverse_root(residual_mid, EPS_NORM)
    ffn_local = (residual_mid * scale_two * ffn_gain).astype(LOW)
    ffn_input = gather_rows(ffn_local, mp_axes)
    if everyone:
        half_rows = lax.dynamic_slice_in_dim(
            ffn_input, lax.axis_index("core") * (group_rows // 2), group_rows // 2, 0
        )
        all_ffn_input = lax.all_gather(half_rows, ("dp", "core"), axis=0, tiled=True)
        grad_rows = lax.dynamic_slice_in_dim(
            all_grad_rows, lax.axis_index("dp") * group_rows, group_rows, 0
        )
    else:
        grad_rows = gather_rows(cotangent, mp_axes)

    hidden_low, d_gate_low, d_up_low = ffn_terms(
        ffn_input, grad_rows, gate_weight, up_weight, down_weight
    )
    d_ffn_norm = scatter_sum(
        dot_full("tf,df->td", d_gate_low, gate_weight) + dot_full("tf,df->td", d_up_low, up_weight),
        mp_axes,
    )
    ffn_part = dot_full("tf,fd->td", hidden_low, down_weight)
    d_ffn = None
    if not everyone:
        d_ffn = (
            dot_full("td,tf->df", ffn_input, d_gate_low),
            dot_full("td,tf->df", ffn_input, d_up_low),
            dot_full("tf,td->fd", hidden_low, grad_rows),
        )

    d_mid = cotangent.astype(FULL) + norm_back(residual_mid, scale_two, ffn_gain, d_ffn_norm)
    ffn_gain_part = jnp.sum(d_ffn_norm * residual_mid * scale_two, axis=0)
    mid_rows = gather_rows(d_mid.astype(LOW), mp_axes)
    mid_rows, ffn_part = lax.optimization_barrier((mid_rows, ffn_part))
    ffn_out = scatter_sum(ffn_part, mp_axes)
    output = (residual_mid + ffn_out).astype(LOW)
    d_output_w = dot_full("tf,td->fd", mixer_low, mid_rows).astype(LOW)
    d_mixer = dot_full("td,fd->tf", mid_rows, output_weight)
    d_gate_low = gate_back(d_mixer, kept[5], projections[3], head_gain)
    d_gating_w = dot_full("td,tf->df", normed, d_gate_low).astype(LOW)
    d_mixer, d_output_w, d_gating_w = lax.optimization_barrier((d_mixer, d_output_w, d_gating_w))
    if everyone:
        d_output_w, d_gating_w = pair_sum(d_output_w), pair_sum(d_gating_w)
    *low_grads, d_logits, d_taps, head_gain_part = run_mixer_backward(
        d_mixer, projections, logits, taps, gain_row, meta, ids, kept
    )
    d_logits = d_logits[:, :head_count]
    d_beta_w = dot_full("td,tf->df", normed, d_logits)
    small = jnp.concatenate([d_beta_w.reshape(-1), d_taps.reshape(-1)])
    size = small.shape[0]
    padded = -(-size // (32 * 512)) * 32 * 512
    small = jnp.pad(small, (0, padded - size)).reshape(-1, 512).astype(LOW)
    narrow = [d_output_w, d_gating_w]
    narrow += [dot_full("td,tf->df", normed, grads).astype(LOW) for grads in low_grads]
    narrow.append(small)
    summed = dot_full("tf,df->td", d_logits, beta_weight)
    for grads, weight in zip(low_grads + [d_gate_low], weights):
        summed = summed + dot_full("tf,df->td", grads, weight)
    if everyone:
        kept_rows, sent_rows = scatter_near(summed)
        sent_rows, *narrow = lax.optimization_barrier((sent_rows, *narrow))
        got_rows = swapped(sent_rows, "y")
        *d_ffn, d_output_w, d_gating_w, d_query_w, d_key_w, d_value_w, small = run_ffn_and_sums(
            all_ffn_input,
            all_grad_rows,
            gate_weight,
            up_weight,
            down_weight,
            narrow,
            (
                (None, 0, 1, 2, 3, 4),
                (None, 1, 2, 3, 4, 5),
                (0, 2, 3, 4, 5, 6),
                (1, 3, 4, 5, 6, 7),
                (2, 4, 5, 6, 7, 8),
                (2, 4, 5, 6, 7, 8),
            ),
        )
        got_rows, small = lax.optimization_barrier((got_rows, small))
        d_normed = kept_rows + got_rows.astype(FULL)
    else:
        d_normed = scatter_sum(summed, mp_axes)
        d_output_w, d_gating_w, d_query_w, d_key_w, d_value_w, small = lax.psum(narrow, "dp")
        d_ffn = lax.psum([grads.astype(LOW) for grads in d_ffn], "dp")
    input_grad = d_mid + norm_back(residual_in, scale_one, norm_gain, d_normed)
    norm_gain_part = jnp.sum(d_normed * residual_in * scale_one, axis=0)
    gains = jnp.concatenate([norm_gain_part, ffn_gain_part, head_gain_part[0]])
    d_gate_w, d_up_w, d_down = [grads.astype(FULL) for grads in d_ffn]
    proj_grads = [grads.astype(FULL) for grads in (d_query_w, d_key_w, d_value_w, d_gating_w)]
    d_output_w = d_output_w.astype(FULL)
    wide = [d_gate_w, d_up_w, d_down, d_output_w] + proj_grads
    place = 0
    for name in (*mp_axes, "dp"):
        count = lax.axis_size(name)
        bit = 1
        while bit < count:
            got = lax.ppermute(gains, name, [(here, here ^ bit) for here in range(count)])
            if place < len(wide):
                got, wide[place] = lax.optimization_barrier((got, wide[place]))
            gains = gains + got
            place, bit = place + 1, 2 * bit
    d_gate_w, d_up_w, d_down, d_output_w, *proj_grads = wide
    small = small.astype(FULL)
    small = small.reshape(-1)
    beta_size, taps_size = d_beta_w.size, taps.size
    d_beta_w = small[:beta_size].reshape(d_beta_w.shape)
    d_conv = small[beta_size : beta_size + taps_size].reshape(conv_weight.shape)
    features = inputs.shape[1]
    return (
        output,
        input_grad,
        gains[:features],
        proj_grads[0],
        proj_grads[1],
        proj_grads[2],
        d_beta_w,
        proj_grads[3],
        d_conv,
        gains[2 * features :],
        d_output_w,
        gains[features : 2 * features],
        d_gate_w,
        d_up_w,
        d_down,
    )


def solution(mesh):
    mp_axes = ("mp",)
    if mesh.shape["mp"] == 4:
        mp_axes = CHIP_AXES
        mesh = jax.sharding.Mesh(mesh.devices.reshape(-1, 2, 2), ("dp", *CHIP_AXES))
    rows, columns, every = P(("dp", *mp_axes), None), P(None, mp_axes), P()
    heads = P(None, None, mp_axes)
    units = P(mp_axes, None)
    return jax.shard_map(
        functools.partial(on_device, mp_axes),
        mesh=mesh,
        in_specs=(rows, P("dp", None), rows, every)
        + (columns,) * 5
        + (heads, every, units, every, columns, columns, units),
        out_specs=(rows, rows, every)
        + (columns,) * 5
        + (heads, every, units, every, columns, columns, units),
        check_vma=False,
    )
```

```python
import functools
import math

import jax
import jax.numpy as jnp
from jax import lax
from jax.experimental import pallas as pl
from jax.experimental.pallas import tpu as pltpu
from jax.sharding import PartitionSpec as P

DK = 128
CONV = 4
SPAN = 128
PAD = 8
ROWS_MOST = 8192


EPS_NORM = 1e-06
EPS_UNIT = 1e-06
EPS_HEAD = 0.05
LOW = jnp.bfloat16
FULL = jnp.float32


def sigmoid(values):
    return 1.0 / (1.0 + jnp.exp(-values))


def parts_of(values):
    high = values.astype(LOW)
    return (high, (values - high.astype(FULL)).astype(LOW))


def product(left, right, left_dim=1, right_dim=0):
    dims = (((left_dim,), (right_dim,)), ((), ()))
    right_free = 1 - right_dim
    width = right[0].shape[right_free]
    if len(left) == 2:
        left_all = jnp.concatenate(left, axis=left_dim)
        first = jnp.concatenate([right[0], right[0]], axis=right_dim)
    else:
        left_all, first = left[0], right[0]
    if len(right) == 1:
        return lax.dot_general(left_all, first, dims, preferred_element_type=FULL)
    second = right[1]
    if len(left) == 2:
        second = jnp.concatenate([second, jnp.zeros_like(second)], axis=right_dim)
    both = lax.dot_general(
        left_all,
        jnp.concatenate([first, second], axis=right_free),
        dims,
        preferred_element_type=FULL,
    )
    return both[:, :width] + both[:, width:]


def lag_rows(stacked, lag_step):
    if lag_step == 0:
        return stacked[PAD:]
    return pltpu.roll(stacked, lag_step, axis=0)[PAD:]


def lead_rows(stacked, lag_step):
    rows = stacked.shape[0]
    if lag_step == 0:
        return stacked[: rows - PAD]
    return pltpu.roll(stacked, rows - lag_step, axis=0)[: rows - PAD]


def with_earlier(ref, start, columns):
    before = pl.multiple_of(jnp.maximum(start - PAD, 0), PAD)
    return jnp.concatenate(
        [ref[pl.ds(before, PAD), columns], ref[pl.ds(start, SPAN), columns]], axis=0
    )


def block_masks(meta_ref, ids_ref, start, index):
    ids_col = meta_ref[pl.ds(start, SPAN), 0:1]
    ids_row = ids_ref[pl.ds(index, 1), :]
    row_ids = lax.broadcasted_iota(jnp.int32, (SPAN, SPAN), 0)
    col_ids = lax.broadcasted_iota(jnp.int32, (SPAN, SPAN), 1)
    same = ids_col == ids_row
    strict = jnp.where(same & (row_ids > col_ids), 1.0, 0.0)
    inclusive = jnp.where(same & (row_ids >= col_ids), 1.0, 0.0)
    return strict, inclusive, row_ids, col_ids


def spread(meta_ref, start, column, rows=SPAN):
    return jnp.broadcast_to(meta_ref[pl.ds(start, rows), column : column + 1], (rows, DK))


def inverse_lower(lower, row_ids, col_ids):
    size = lower.shape[0]
    step = 1
    result = jnp.where(row_ids == col_ids, 1.0, 0.0)
    while step < size:
        pair = (row_ids // (2 * step) == col_ids // (2 * step)) & (
            row_ids // step != col_ids // step
        )
        link = jnp.where(pair, lower, 0.0)
        if step == 1:
            result = result - link
        else:
            result_parts = parts_of(result)
            inner = product(parts_of(link), result_parts)
            yield
            result = result - product(result_parts, parts_of(inner))
            yield
        step = 2 * step
    return result


def side_by_side(works):
    works = list(works)
    while works:
        left = []
        for work in works:
            try:
                next(work)
                left.append(work)
            except StopIteration:
                pass
        works = left


def mixer_forward(
    head_count,
    query_ref,
    key_ref,
    value_ref,
    gate_ref,
    logit_ref,
    taps_ref,
    gain_ref,
    meta_ref,
    ids_ref,
    mixer_ref,
    conv_ref,
    solve_ref,
    w_ref,
    u_ref,
    new_ref,
    mixed_ref,
    states_ref,
    state,
):
    state[...] = jnp.zeros_like(state)
    gain = gain_ref[...]

    def step(index, carry):
        start = pl.multiple_of(index * SPAN, SPAN)
        rows = pl.ds(start, SPAN)
        strict, inclusive, row_ids, col_ids = block_masks(meta_ref, ids_ref, start, index)
        tap_masks = [None] + [spread(meta_ref, start, lag_step) for lag_step in range(1, CONV)]
        opening = spread(meta_ref, start, 4)
        closing = spread(meta_ref, start, 5)
        carried = spread(meta_ref, start, 6)
        betas = sigmoid(logit_ref[rows, :])
        def work(head):
            columns = slice(head * DK, (head + 1) * DK)
            acts = []
            for which, ref in enumerate((query_ref, key_ref, value_ref)):
                stacked = with_earlier(ref, start, columns)
                tap = 4 * which
                total = taps_ref[tap : tap + 1, columns] * lag_rows(stacked, 0)
                for lag_step in range(1, CONV):
                    total = total + (
                        taps_ref[tap + lag_step : tap + lag_step + 1, columns]
                        * lag_rows(stacked, lag_step)
                        * tap_masks[lag_step]
                    )
                conv_ref[which, rows, columns] = total
                acts.append(total * sigmoid(total))
            unit = [
                act * lax.rsqrt(jnp.sum(act * act, axis=-1, keepdims=True) + EPS_UNIT)
                for act in acts[:2]
            ]
            queries, keys, values = unit[0].astype(LOW), unit[1].astype(LOW), acts[2].astype(LOW)
            yield
            beta = jnp.broadcast_to(betas[:, head : head + 1], (SPAN, DK))
            gram = product((keys,), (keys,), 1, 1)
            yield
            solve = yield from inverse_lower(beta * gram * strict, row_ids, col_ids)
            solve_ref[head, rows, :] = solve
            solve_parts = parts_of(solve)
            w_rows = product(solve_parts, parts_of(beta * keys.astype(FULL)))
            u_rows = product(solve_parts, parts_of(beta * values.astype(FULL)))
            w_ref[rows, columns] = w_rows
            u_ref[rows, columns] = u_rows
            yield
            probes = product((queries,), (keys,), 1, 1) * inclusive
            before = state[head]
            states_ref[head, rows, :] = before
            before_parts = parts_of(before)
            new_value = u_rows - opening * product(parts_of(w_rows), before_parts)
            new_ref[rows, columns] = new_value
            yield
            mixed = opening * product((queries,), before_parts) + product(
                parts_of(probes), parts_of(new_value)
            )
            mixed_ref[rows, columns] = mixed
            yield
            state[head] = carried * before + product(
                (keys,), parts_of(closing * new_value), 0, 0
            )
            scale = lax.rsqrt(jnp.mean(mixed * mixed, axis=-1, keepdims=True) + EPS_HEAD)
            gates = gate_ref[rows, columns]
            mixer_ref[rows, columns] = (mixed * scale * gain * (gates * sigmoid(gates))).astype(LOW)

        side_by_side(work(head) for head in range(head_count))
        return carry

    lax.fori_loop(0, query_ref.shape[0] // SPAN, step, 0)


def mixer_backward(
    head_count,
    d_mixer_ref,
    query_ref,
    key_ref,
    value_ref,
    gate_ref,
    logit_ref,
    taps_ref,
    gain_ref,
    meta_ref,
    ids_ref,
    conv_ref,
    solve_ref,
    w_ref,
    u_ref,
    new_ref,
    mixed_ref,
    states_ref,
    d_query_ref,
    d_key_ref,
    d_value_ref,
    d_logit_ref,
    d_taps_ref,
    d_gain_ref,
    d_state,
    later,
):
    d_state[...] = jnp.zeros_like(d_state)
    later[...] = jnp.zeros_like(later)
    d_taps_ref[...] = jnp.zeros_like(d_taps_ref)
    d_gain_ref[...] = jnp.zeros_like(d_gain_ref)
    gain = gain_ref[...]
    total_rows = query_ref.shape[0]
    count = total_rows // SPAN

    def step(back, carry):
        index = count - 1 - back
        start = pl.multiple_of(index * SPAN, SPAN)
        rows = pl.ds(start, SPAN)
        strict, inclusive, row_ids, col_ids = block_masks(meta_ref, ids_ref, start, index)
        after = pl.multiple_of(jnp.minimum(start + SPAN, total_rows - PAD), PAD)
        tap_masks = [None] + [
            jnp.concatenate(
                [
                    spread(meta_ref, start, lag_step),
                    spread(meta_ref, after, lag_step, PAD),
                ],
                axis=0,
            )
            for lag_step in range(1, CONV)
        ]
        opening = spread(meta_ref, start, 4)
        closing = spread(meta_ref, start, 5)
        carried = spread(meta_ref, start, 6)
        betas = sigmoid(logit_ref[rows, :])
        lanes = lax.broadcasted_iota(jnp.int32, (SPAN, DK), 1)
        d_logits = jnp.zeros((SPAN, DK), FULL)
        d_gain = jnp.zeros((1, DK), FULL)
        def work(head):
            nonlocal d_gain, d_logits
            columns = slice(head * DK, (head + 1) * DK)
            d_mixer = d_mixer_ref[rows, columns]
            gates = gate_ref[rows, columns]
            logistic = sigmoid(gates)
            mixed = mixed_ref[rows, columns]
            scale = lax.rsqrt(jnp.mean(mixed * mixed, axis=-1, keepdims=True) + EPS_HEAD)
            unit_mixed = mixed * scale
            d_normed = d_mixer * (gates * logistic)
            d_gain = d_gain + jnp.sum(d_normed * unit_mixed, axis=0, keepdims=True)
            weighted = d_normed * gain
            inner = jnp.mean(weighted * mixed, axis=-1, keepdims=True)
            d_out = scale * weighted - mixed * (scale * scale * scale) * inner
            yield
            convs = [conv_ref[which, rows, columns] for which in range(3)]
            logistics = [sigmoid(conv) for conv in convs]
            acts = [conv * logistic for conv, logistic in zip(convs, logistics)]
            scales = [
                lax.rsqrt(jnp.sum(act * act, axis=-1, keepdims=True) + EPS_UNIT)
                for act in acts[:2]
            ]
            queries = (acts[0] * scales[0]).astype(LOW)
            keys = (acts[1] * scales[1]).astype(LOW)
            values = acts[2].astype(LOW)
            beta = jnp.broadcast_to(betas[:, head : head + 1], (SPAN, DK))
            gram = product((keys,), (keys,), 1, 1)
            probes = product((queries,), (keys,), 1, 1) * inclusive
            solve_parts = parts_of(solve_ref[head, rows, :])
            w_parts = parts_of(w_ref[rows, columns])
            u_parts = parts_of(u_ref[rows, columns])
            new_value = new_ref[rows, columns]
            new_parts = parts_of(new_value)
            before_parts = parts_of(states_ref[head, rows, :])
            yield
            d_after = d_state[head]
            d_after_parts = parts_of(d_after)
            d_out_parts = parts_of(d_out)
            d_new = product(parts_of(probes), d_out_parts, 0, 0) + closing * product(
                (keys,), d_after_parts
            )
            yield
            opened_out = opening * d_out
            opened_new = opening * d_new
            d_state[head] = (
                carried * d_after
                + product((queries,), parts_of(opened_out), 0, 0)
                - product(w_parts, parts_of(opened_new), 0, 0)
            )
            yield
            d_probe = product(d_out_parts, new_parts, 1, 1) * inclusive
            d_probe_parts = parts_of(d_probe)
            yield
            d_query = product(d_probe_parts, (keys,)) + product(
                parts_of(opened_out), before_parts, 1, 1
            )
            yield
            d_key = product(d_probe_parts, (queries,), 0, 0) + closing * product(
                new_parts, d_after_parts, 1, 1
            )
            yield
            d_w = -product(parts_of(opened_new), before_parts, 1, 1)
            yield
            right_w = product(solve_parts, parts_of(d_w), 0, 0)
            right_u = product(solve_parts, parts_of(d_new), 0, 0)
            yield
            d_lower = (
                -(
                    product(parts_of(right_w), w_parts, 1, 1)
                    + product(parts_of(right_u), u_parts, 1, 1)
                )
                * strict
            )
            yield
            d_beta = jnp.sum(
                right_w * keys.astype(FULL) + right_u * values.astype(FULL) + d_lower * gram,
                axis=-1,
                keepdims=True,
            )
            beta_col = betas[:, head : head + 1]
            d_logits = d_logits + jnp.where(
                lanes == head, d_beta * beta_col * (1.0 - beta_col), 0.0
            )
            yield
            d_gram_parts = parts_of(beta * d_lower)
            d_key = (
                d_key
                + beta * right_w
                + product(d_gram_parts, (keys,))
                + product(d_gram_parts, (keys,), 0, 0)
            )
            yield
            d_value = beta * right_u
            yield
            d_acts = [
                scales[which] * grads
                - acts[which]
                * (scales[which] * scales[which] * scales[which])
                * jnp.sum(grads * acts[which], axis=-1, keepdims=True)
                for which, grads in enumerate((d_query, d_key))
            ] + [d_value]
            for which, (ref, out_ref) in enumerate(
                ((query_ref, d_query_ref), (key_ref, d_key_ref), (value_ref, d_value_ref))
            ):
                logistic = logistics[which]
                d_conv = d_acts[which] * (logistic * (1.0 + convs[which] * (1.0 - logistic)))
                tap = 4 * which
                following = jnp.concatenate([d_conv, later[which, :, columns]], axis=0)
                earlier = with_earlier(ref, start, columns)
                later[which, :, columns] = d_conv[:PAD]
                total = taps_ref[tap : tap + 1, columns] * d_conv
                d_taps = [jnp.sum(d_conv * lag_rows(earlier, 0), axis=0, keepdims=True)]
                for lag_step in range(1, CONV):
                    masked = following * tap_masks[lag_step]
                    total = total + taps_ref[
                        tap + lag_step : tap + lag_step + 1, columns
                    ] * lead_rows(masked, lag_step)
                    d_taps.append(
                        jnp.sum(
                            masked[:SPAN] * lag_rows(earlier, lag_step), axis=0, keepdims=True
                        )
                    )
                out_ref[rows, columns] = total.astype(LOW)
                for lag_step in range(CONV):
                    place = slice(tap + lag_step, tap + lag_step + 1)
                    d_taps_ref[place, columns] = d_taps_ref[place, columns] + d_taps[lag_step]

        side_by_side(work(head) for head in range(head_count))
        d_logit_ref[rows, :] = d_logits.astype(LOW)
        d_gain_ref[...] = d_gain_ref[...] + d_gain
        return carry

    lax.fori_loop(0, count, step, 0)


def whole_blocks(count):
    return [pl.BlockSpec(memory_space=pltpu.VMEM)] * count


def run_mixer_forward(projections, logits, taps, gain, meta, ids):
    rows, width = projections[0].shape
    head_count = width // DK
    tall = jax.ShapeDtypeStruct((rows, width), FULL)
    square = jax.ShapeDtypeStruct((head_count, rows, DK), FULL)
    return pl.pallas_call(
        functools.partial(mixer_forward, head_count),
        out_shape=(
            jax.ShapeDtypeStruct((rows, width), LOW),
            jax.ShapeDtypeStruct((3, rows, width), FULL),
            square,
            tall,
            tall,
            tall,
            tall,
            square,
        ),
        in_specs=whole_blocks(9),
        out_specs=tuple(whole_blocks(8)),
        scratch_shapes=[pltpu.VMEM((head_count, DK, DK), FULL)],
        compiler_params=pltpu.CompilerParams(vmem_limit_bytes=56 * 1024 * 1024),
        name="mixer_forward",
    )(*projections, logits, taps, gain, meta, ids)


def run_mixer_backward(d_mixer, projections, logits, taps, gain, meta, ids, kept):
    rows, width = projections[0].shape
    head_count = width // DK
    low = jax.ShapeDtypeStruct((rows, width), LOW)
    return pl.pallas_call(
        functools.partial(mixer_backward, head_count),
        out_shape=(
            low,
            low,
            low,
            jax.ShapeDtypeStruct((rows, DK), LOW),
            jax.ShapeDtypeStruct(taps.shape, FULL),
            jax.ShapeDtypeStruct((1, DK), FULL),
        ),
        in_specs=whole_blocks(17),
        out_specs=tuple(whole_blocks(6)),
        scratch_shapes=[
            pltpu.VMEM((head_count, DK, DK), FULL),
            pltpu.VMEM((3, PAD, width), FULL),
        ],
        compiler_params=pltpu.CompilerParams(vmem_limit_bytes=56 * 1024 * 1024),
        name="mixer_backward",
    )(d_mixer, *projections, logits, taps, gain, meta, ids, *kept)


def document_tables(doc_ids):
    rows = doc_ids.shape[0]
    columns = [doc_ids.astype(FULL)]
    for lag_step in range(1, CONV):
        before = jnp.concatenate(
            [jnp.full((lag_step,), -1, jnp.int32), doc_ids[: rows - lag_step]]
        )
        columns.append((doc_ids == before).astype(FULL))
    blocks = doc_ids.reshape(rows // SPAN, SPAN)
    prior = jnp.concatenate([jnp.full((1,), -1, jnp.int32), blocks[:-1, SPAN - 1]])[:, None]
    last = blocks[:, SPAN - 1 :]
    columns.append((blocks == prior).astype(FULL).reshape(-1))
    columns.append((blocks == last).astype(FULL).reshape(-1))
    columns.append(jnp.broadcast_to(last == prior, blocks.shape).astype(FULL).reshape(-1))
    columns.append(jnp.zeros((rows,), FULL))
    return jnp.stack(columns, axis=1), blocks.astype(FULL)


def mm(left, right, left_dim, right_dim):
    return lax.dot_general(
        left, right, (((left_dim,), (right_dim,)), ((), ())), preferred_element_type=FULL
    )


FFN_TILE = 128
FFN_ROWS = 1024
TICKS = 9
X_SENT, X_GOT, OWN, IN_SENT, IN_GOT, MID_SENT, MID_GOT, OUT_SENT, OUT_GOT, BACK_SENT, BACK_GOT, KEPT = range(12)


def add_into(target_ref, other_ref):
    rows = target_ref.shape[0]
    piece = min(rows, 128)

    def add(index, carry):
        place = pl.ds(pl.multiple_of(index * piece, piece), piece)
        target_ref[place, :] = (
            target_ref[place, :].astype(FULL) + other_ref[place, :].astype(FULL)
        ).astype(LOW)
        return carry

    lax.fori_loop(0, rows // piece, add, 0)


def ffn_step(rows_ref, grads_ref, gate_ref, up_ref, down_ref, d_gate_ref, d_up_ref, d_down_ref, total):
    block, tile = pl.program_id(1), gate_ref.shape[1]

    @pl.when(block == 0)
    def _():
        total[...] = jnp.zeros_like(total)

    rows, grads = rows_ref[...], grads_ref[...]
    both = mm(rows, jnp.concatenate([gate_ref[...], up_ref[...]], axis=1), 1, 0)
    gate_pre, up_pre = both[:, :tile], both[:, tile:]
    d_hidden = mm(grads, down_ref[...], 1, 1)
    logistic = sigmoid(gate_pre)
    gate_swish = gate_pre * logistic
    hidden_low = (gate_swish * up_pre).astype(LOW)
    d_gate_low = (d_hidden * up_pre * (logistic * (1.0 + gate_pre * (1.0 - logistic)))).astype(LOW)
    d_up_low = (d_hidden * gate_swish).astype(LOW)
    total[: 2 * tile] += mm(jnp.concatenate([d_gate_low, d_up_low], axis=1), rows, 0, 0)
    total[2 * tile :] += mm(hidden_low, grads, 0, 0)

    @pl.when(block == pl.num_programs(1) - 1)
    def _():
        d_gate_ref[...] = total[:tile].T.astype(LOW)
        d_up_ref[...] = total[tile : 2 * tile].T.astype(LOW)
        d_down_ref[...] = total[2 * tile :].astype(LOW)


def ffn_and_sums(plans, ticks, *refs):
    count = len(plans)
    ffn_refs, given = refs[:5], refs[5 : 5 + count]
    d_refs, made = refs[5 + count : 8 + count], refs[8 + count : 8 + 2 * count]
    scratch = refs[8 + 2 * count :]
    total, sems = scratch[0], scratch[1]
    halves, owns, ins, mids = (
        scratch[2 + kind * count : 2 + (kind + 1) * count] for kind in range(4)
    )
    step = pl.program_id(0) * pl.num_programs(1) + pl.program_id(1)
    here = lax.axis_index("dp")
    side, place = here % 2, here // 2
    pair = here + 1 - 2 * side
    near = 2 * (place + 1 - 2 * (place % 2)) + side
    far = 2 * (3 - place) + side
    middle = (place == 1) | (place == 2)
    end = (place == 0) | (place == 3)

    @pl.when(step == 0)
    def _():
        barrier = pltpu.get_barrier_semaphore()
        pl.semaphore_signal(barrier, inc=1, device_id={"dp": pair})
        pl.semaphore_signal(barrier, inc=1, device_id={"dp": near})

        @pl.when(middle)
        def _():
            pl.semaphore_signal(barrier, inc=1, device_id={"dp": far})
            pl.semaphore_wait(barrier, 3)

        @pl.when(end)
        def _():
            pl.semaphore_wait(barrier, 2)

    def plan(which):
        rows = halves[which].shape[0]
        mine = pl.ds(pl.multiple_of(side * rows, rows), rows)
        theirs = pl.ds(pl.multiple_of((1 - side) * rows, rows), rows)

        def remote(source, target, sent, got, device):
            return pltpu.make_async_remote_copy(
                src_ref=source,
                dst_ref=target,
                send_sem=sems.at[which, sent],
                recv_sem=sems.at[which, got],
                device_id={"dp": device},
            )

        def local(source, target, sem):
            return pltpu.make_async_copy(source, target, sems.at[which, sem])

        return dict(
            across=lambda: remote(given[which].at[theirs], halves[which], X_SENT, X_GOT, pair),
            own=lambda: local(given[which].at[mine], owns[which], OWN),
            whole=lambda: local(given[which], halves[which], OWN),
            inward=lambda: remote(halves[which], ins[which], IN_SENT, IN_GOT, near),
            middle=lambda: remote(halves[which], mids[which], MID_SENT, MID_GOT, far),
            outward=lambda: remote(halves[which], made[which].at[mine], OUT_SENT, OUT_GOT, near),
            back_end=lambda: remote(made[which].at[mine], made[which].at[mine], BACK_SENT, BACK_GOT, pair),
            back_middle=lambda: remote(halves[which], made[which].at[mine], BACK_SENT, BACK_GOT, pair),
            back_got=lambda: remote(made[which].at[theirs], made[which].at[theirs], BACK_SENT, BACK_GOT, pair),
            kept=lambda: local(halves[which], made[which].at[mine], KEPT),
        )

    def stage(which, number):
        copies = plan(which)
        if number == 0:
            copies["across"]().start()
            copies["own"]().start()
        elif number == 1:
            if plans[which][0] is None:
                copies["whole"]().start()
                copies["whole"]().wait()
            else:
                copies["own"]().wait()
                copies["across"]().wait()
                add_into(halves[which], owns[which])

            @pl.when(end)
            def _():
                copies["inward"]().start()
        elif number == 2:

            @pl.when(end)
            def _():
                copies["inward"]().wait_send()

            @pl.when(middle)
            def _():
                copies["inward"]().wait_recv()
                add_into(halves[which], ins[which])
                copies["middle"]().start()
        elif number == 3:

            @pl.when(middle)
            def _():
                copies["middle"]().wait()
                add_into(halves[which], mids[which])
                copies["outward"]().start()
                copies["back_middle"]().start()
                copies["kept"]().start()
        elif number == 4:

            @pl.when(end)
            def _():
                copies["outward"]().wait_recv()
                copies["back_end"]().start()

            @pl.when(middle)
            def _():
                copies["outward"]().wait_send()
                copies["kept"]().wait()
        else:

            @pl.when(end)
            def _():
                copies["back_end"]().wait_send()

            @pl.when(middle)
            def _():
                copies["back_middle"]().wait_send()
            copies["back_got"]().wait_recv()

    for tick in range(TICKS):

        @pl.when(step == ticks[tick])
        def _(tick=tick):
            for which, places in enumerate(plans):
                if tick in places:
                    stage(which, places.index(tick))

    ffn_step(*ffn_refs, *d_refs, total)


def run_ffn_and_sums(rows, grads, gate_weight, up_weight, down_weight, given, plans):
    total_rows, features = rows.shape
    units = gate_weight.shape[1]
    block_rows = min(FFN_ROWS, total_rows)
    blocks, tiles = total_rows // block_rows, units // FFN_TILE
    steps = blocks * tiles
    ticks = [((steps - 1) * tick) // (TICKS - 1) for tick in range(TICKS)]
    across = pl.BlockSpec((features, FFN_TILE), lambda tile, block: (0, tile))
    down = pl.BlockSpec((FFN_TILE, features), lambda tile, block: (tile, 0))
    tall = pl.BlockSpec((block_rows, features), lambda tile, block: (block, 0))
    anywhere = [pl.BlockSpec(memory_space=pl.ANY)] * len(given)
    half_shapes = [
        values.shape if places[0] is None else (values.shape[0] // 2, values.shape[1])
        for values, places in zip(given, plans)
    ]
    own_shapes = [
        (16, 128) if places[0] is None else shape for shape, places in zip(half_shapes, plans)
    ]
    return pl.pallas_call(
        functools.partial(ffn_and_sums, plans, ticks),
        grid=(tiles, blocks),
        in_specs=[tall, tall, across, across, down] + anywhere,
        out_specs=[across, across, down] + anywhere,
        out_shape=[
            jax.ShapeDtypeStruct((features, units), LOW),
            jax.ShapeDtypeStruct((features, units), LOW),
            jax.ShapeDtypeStruct((units, features), LOW),
        ]
        + [jax.ShapeDtypeStruct((2 * rows, width), LOW) for rows, width in half_shapes],
        scratch_shapes=[
            pltpu.VMEM((3 * FFN_TILE, features), FULL),
            pltpu.SemaphoreType.DMA((len(given), 12)),
        ]
        + [
            pltpu.VMEM(shape, LOW)
            for shape in half_shapes + own_shapes + half_shapes + half_shapes
        ],
        compiler_params=pltpu.CompilerParams(
            vmem_limit_bytes=60 * 1024 * 1024, collective_id=0, has_side_effects=True
        ),
        cost_estimate=pl.CostEstimate(
            flops=12 * total_rows * features * units,
            bytes_accessed=4 * tiles * total_rows * features,
            transcendentals=total_rows * units,
        ),
        name="ffn_and_sums",
    )(rows, grads, gate_weight, up_weight, down_weight, *given)


CHIP_AXES = ("y", "core")


def swapped(values, name):
    return lax.ppermute(values, name, [(0, 1), (1, 0)])


def gather_rows(values, mp_axes):
    if mp_axes != CHIP_AXES:
        return lax.all_gather(values, mp_axes, axis=0, tiled=True)
    other_core = swapped(values, "core")
    other_chip = swapped(values, "y")
    far = swapped(other_chip, "core")
    odd_core, odd_chip = lax.axis_index("core") == 1, lax.axis_index("y") == 1
    near_pair = jnp.where(
        odd_core,
        jnp.concatenate([other_core, values]),
        jnp.concatenate([values, other_core]),
    )
    far_pair = jnp.where(
        odd_core, jnp.concatenate([far, other_chip]), jnp.concatenate([other_chip, far])
    )
    return jnp.where(
        odd_chip, jnp.concatenate([far_pair, near_pair]), jnp.concatenate([near_pair, far_pair])
    )


def scatter_near(values):
    core, chip = lax.axis_index("core"), lax.axis_index("y")
    quarters = values.reshape(2, 2, values.shape[0] // 4, values.shape[1])
    sent = lax.dynamic_index_in_dim(quarters, 1 - core, 1, keepdims=False).astype(LOW)
    kept = lax.dynamic_index_in_dim(quarters, core, 1, keepdims=False)
    halves = kept + swapped(sent, "core").astype(FULL)
    sent = lax.dynamic_index_in_dim(halves, 1 - chip, 0, keepdims=False).astype(LOW)
    return lax.dynamic_index_in_dim(halves, chip, 0, keepdims=False), sent


def scatter_sum(values, mp_axes):
    if mp_axes != CHIP_AXES:
        return lax.psum_scatter(values, mp_axes, scatter_dimension=0, tiled=True)
    kept, sent = scatter_near(values)
    return kept + swapped(sent, "y").astype(FULL)


def half_of(values, which):
    size = values.shape[0] // 2
    return lax.dynamic_slice_in_dim(values, which * size, size, 0)


def pair_sum(values):
    side = lax.axis_index("dp") % 2
    sent = lax.ppermute(half_of(values, 1 - side), "dp", [(here, here ^ 1) for here in range(8)])
    return (half_of(values, side).astype(FULL) + sent.astype(FULL)).astype(LOW)


def inverse_root(values, epsilon):
    return lax.rsqrt(jnp.mean(values * values, axis=-1, keepdims=True) + epsilon)


def norm_back(values, scales, gains, grads):
    weighted = grads * gains
    inner_sum = jnp.mean(weighted * values, axis=-1, keepdims=True)
    return scales * weighted - values * (scales * scales * scales) * inner_sum


def sigmoid_linear(values):
    return values * sigmoid(values)


def sigmoid_slope(values):
    logistic = sigmoid(values)
    return logistic * (1.0 + values * (1.0 - logistic))


def gate_back(d_mixer, mixed, gates, head_gain):
    shape = mixed.shape
    heads = mixed.reshape(shape[0], shape[1] // DK, DK)
    normed = (heads * inverse_root(heads, EPS_HEAD) * head_gain).reshape(shape)
    return (d_mixer * normed * sigmoid_slope(gates)).astype(LOW)


def doc_index(lengths, length):
    starts = jnp.cumsum(lengths, axis=1) - lengths
    places = jnp.arange(length, dtype=jnp.int32)
    within = jnp.sum((starts[:, :, None] <= places[None, None, :]).astype(jnp.int32), axis=1) - 1
    offsets = jnp.arange(lengths.shape[0], dtype=jnp.int32)[:, None] * lengths.shape[1]
    return (within + offsets).reshape(-1)


def dot_full(equation, left, right):
    return jnp.einsum(equation, left, right, preferred_element_type=FULL)


def ffn_terms(rows, grad_rows, gate_weight, up_weight, down_weight):
    gate_pre = dot_full("td,df->tf", rows, gate_weight)
    up_pre = dot_full("td,df->tf", rows, up_weight)
    d_hidden = dot_full("td,fd->tf", grad_rows, down_weight)
    gate_swish = sigmoid_linear(gate_pre)
    hidden_low = (gate_swish * up_pre).astype(LOW)
    d_gate_low = (d_hidden * up_pre * sigmoid_slope(gate_pre)).astype(LOW)
    d_up_low = (d_hidden * gate_swish).astype(LOW)
    return hidden_low, d_gate_low, d_up_low


def on_device(
    mp_axes,
    inputs,
    doc_lengths,
    cotangent,
    norm_gain,
    query_weight,
    key_weight,
    value_weight,
    beta_weight,
    gating_weight,
    conv_weight,
    head_gain,
    output_weight,
    ffn_gain,
    gate_weight,
    up_weight,
    down_weight,
):
    local_rows = inputs.shape[0]
    group_rows = local_rows * math.prod(lax.axis_size(name) for name in mp_axes)
    width = query_weight.shape[1]
    head_count = width // DK
    meta, ids = document_tables(doc_index(doc_lengths, group_rows // doc_lengths.shape[0]))
    taps = conv_weight.reshape(3 * CONV, width)
    gain_row = head_gain[None, :]

    everyone = (
        mp_axes == CHIP_AXES
        and lax.axis_size("dp") == 8
        and group_rows * lax.axis_size("dp") <= ROWS_MOST
    )
    if everyone:
        all_grad_rows = lax.all_gather(cotangent, ("dp", *mp_axes), axis=0, tiled=True)
    residual_in = inputs.astype(FULL)
    scale_one = inverse_root(residual_in, EPS_NORM)
    normed = gather_rows((residual_in * scale_one * norm_gain).astype(LOW), mp_axes)
    weights = (query_weight, key_weight, value_weight, gating_weight)
    projections = tuple(dot_full("td,df->tf", normed, weight) for weight in weights)
    logits = dot_full("td,df->tf", normed, beta_weight)
    mixer_low, *kept = run_mixer_forward(projections, logits, taps, gain_row, meta, ids)
    attended = scatter_sum(dot_full("tf,fd->td", mixer_low, output_weight), mp_axes)
    residual_mid = residual_in + attended
    scale_two = inverse_root(residual_mid, EPS_NORM)
    ffn_local = (residual_mid * scale_two * ffn_gain).astype(LOW)
    ffn_input = gather_rows(ffn_local, mp_axes)
    if everyone:
        half_rows = lax.dynamic_slice_in_dim(
            ffn_input, lax.axis_index("core") * (group_rows // 2), group_rows // 2, 0
        )
        all_ffn_input = lax.all_gather(half_rows, ("dp", "core"), axis=0, tiled=True)
        grad_rows = lax.dynamic_slice_in_dim(
            all_grad_rows, lax.axis_index("dp") * group_rows, group_rows, 0
        )
    else:
        grad_rows = gather_rows(cotangent, mp_axes)

    hidden_low, d_gate_low, d_up_low = ffn_terms(
        ffn_input, grad_rows, gate_weight, up_weight, down_weight
    )
    d_ffn_norm = scatter_sum(
        dot_full("tf,df->td", d_gate_low, gate_weight) + dot_full("tf,df->td", d_up_low, up_weight),
        mp_axes,
    )
    d_ffn = None
    if not everyone:
        d_ffn = (
            dot_full("td,tf->df", ffn_input, d_gate_low),
            dot_full("td,tf->df", ffn_input, d_up_low),
            dot_full("tf,td->fd", hidden_low, grad_rows),
        )

    d_mid = cotangent.astype(FULL) + norm_back(residual_mid, scale_two, ffn_gain, d_ffn_norm)
    ffn_gain_part = jnp.sum(d_ffn_norm * residual_mid * scale_two, axis=0)
    mid_rows = gather_rows(d_mid.astype(LOW), mp_axes)
    d_output_w = dot_full("tf,td->fd", mixer_low, mid_rows).astype(LOW)
    d_mixer = dot_full("td,fd->tf", mid_rows, output_weight)
    d_gate_low = gate_back(d_mixer, kept[5], projections[3], head_gain)
    d_gating_w = dot_full("td,tf->df", normed, d_gate_low).astype(LOW)
    d_mixer, d_output_w, d_gating_w = lax.optimization_barrier((d_mixer, d_output_w, d_gating_w))
    if everyone:
        d_output_w, d_gating_w = pair_sum(d_output_w), pair_sum(d_gating_w)
    *low_grads, d_logits, d_taps, head_gain_part = run_mixer_backward(
        d_mixer, projections, logits, taps, gain_row, meta, ids, kept
    )
    d_logits, hidden_low = lax.optimization_barrier((d_logits, hidden_low))
    ffn_out = scatter_sum(dot_full("tf,fd->td", hidden_low, down_weight), mp_axes)
    output = (residual_mid + ffn_out).astype(LOW)
    d_logits = d_logits[:, :head_count]
    d_beta_w = dot_full("td,tf->df", normed, d_logits)
    small = jnp.concatenate([d_beta_w.reshape(-1), d_taps.reshape(-1)])
    size = small.shape[0]
    padded = -(-size // (32 * 512)) * 32 * 512
    small = jnp.pad(small, (0, padded - size)).reshape(-1, 512).astype(LOW)
    narrow = [d_output_w, d_gating_w]
    narrow += [dot_full("td,tf->df", normed, grads).astype(LOW) for grads in low_grads]
    narrow.append(small)
    summed = dot_full("tf,df->td", d_logits, beta_weight)
    for grads, weight in zip(low_grads + [d_gate_low], weights):
        summed = summed + dot_full("tf,df->td", grads, weight)
    if everyone:
        kept_rows, sent_rows = scatter_near(summed)
        sent_rows, *narrow = lax.optimization_barrier((sent_rows, *narrow))
        got_rows = swapped(sent_rows, "y")
        *d_ffn, d_output_w, d_gating_w, d_query_w, d_key_w, d_value_w, small = run_ffn_and_sums(
            all_ffn_input,
            all_grad_rows,
            gate_weight,
            up_weight,
            down_weight,
            narrow,
            (
                (None, 0, 1, 2, 3, 4),
                (None, 1, 2, 3, 4, 5),
                (0, 2, 3, 4, 5, 6),
                (1, 3, 4, 5, 6, 7),
                (2, 4, 5, 6, 7, 8),
                (2, 4, 5, 6, 7, 8),
            ),
        )
        got_rows, small = lax.optimization_barrier((got_rows, small))
        d_normed = kept_rows + got_rows.astype(FULL)
    else:
        d_normed = scatter_sum(summed, mp_axes)
        d_output_w, d_gating_w, d_query_w, d_key_w, d_value_w, small = lax.psum(narrow, "dp")
        d_ffn = lax.psum([grads.astype(LOW) for grads in d_ffn], "dp")
    input_grad = d_mid + norm_back(residual_in, scale_one, norm_gain, d_normed)
    norm_gain_part = jnp.sum(d_normed * residual_in * scale_one, axis=0)
    gains = jnp.concatenate([norm_gain_part, ffn_gain_part, head_gain_part[0]])
    d_gate_w, d_up_w, d_down = [grads.astype(FULL) for grads in d_ffn]
    proj_grads = [grads.astype(FULL) for grads in (d_query_w, d_key_w, d_value_w, d_gating_w)]
    d_output_w = d_output_w.astype(FULL)
    wide = [d_gate_w, d_up_w, d_down, d_output_w] + proj_grads
    place = 0
    for name in (*mp_axes, "dp"):
        count = lax.axis_size(name)
        bit = 1
        while bit < count:
            got = lax.ppermute(gains, name, [(here, here ^ bit) for here in range(count)])
            if place < len(wide):
                got, wide[place] = lax.optimization_barrier((got, wide[place]))
            gains = gains + got
            place, bit = place + 1, 2 * bit
    d_gate_w, d_up_w, d_down, d_output_w, *proj_grads = wide
    small = small.astype(FULL)
    small = small.reshape(-1)
    beta_size, taps_size = d_beta_w.size, taps.size
    d_beta_w = small[:beta_size].reshape(d_beta_w.shape)
    d_conv = small[beta_size : beta_size + taps_size].reshape(conv_weight.shape)
    features = inputs.shape[1]
    return (
        output,
        input_grad,
        gains[:features],
        proj_grads[0],
        proj_grads[1],
        proj_grads[2],
        d_beta_w,
        proj_grads[3],
        d_conv,
        gains[2 * features :],
        d_output_w,
        gains[features : 2 * features],
        d_gate_w,
        d_up_w,
        d_down,
    )


def solution(mesh):
    mp_axes = ("mp",)
    if mesh.shape["mp"] == 4:
        mp_axes = CHIP_AXES
        mesh = jax.sharding.Mesh(mesh.devices.reshape(-1, 2, 2), ("dp", *CHIP_AXES))
    rows, columns, every = P(("dp", *mp_axes), None), P(None, mp_axes), P()
    heads = P(None, None, mp_axes)
    units = P(mp_axes, None)
    return jax.shard_map(
        functools.partial(on_device, mp_axes),
        mesh=mesh,
        in_specs=(rows, P("dp", None), rows, every)
        + (columns,) * 5
        + (heads, every, units, every, columns, columns, units),
        out_specs=(rows, rows, every)
        + (columns,) * 5
        + (heads, every, units, every, columns, columns, units),
        check_vma=False,
    )
```
